32 devices in a mesh: clips: 2 (over y), tile: 4 (over x, core), tm: 4 (over z).
Axes of the slice: x: 2, y: 2, z: 4, core: 2. Of those that a mesh axis runs over, the one named last changes fastest.
Arguments:
- frames: bfloat16 [8, 120, 32, 128], P(('clips', 'tm'), None, 'tile'), parts along dimension 0, may hold values from -6 to 6
- ln_gain: float32 [2, 2, 120], replicated, may hold values from 0.5 to 1.5
- qkv_weight: bfloat16 [2, 120, 360], replicated, may hold values from -4 to 4
- out_weight: bfloat16 [2, 120, 120], replicated, may hold values from -0.5 to 0.5
- gate_weight: bfloat16 [2, 120, 240], replicated, may hold values from -0.5 to 0.5
- up_weight: bfloat16 [2, 120, 240], replicated, may hold values from -0.5 to 0.5
- down_weight: bfloat16 [2, 240, 120], replicated, may hold values from -0.375 to 0.375
- conv_weight: bfloat16 [2, 9, 120, 120], replicated, may hold values from -0.1875 to 0.1875
- conv_bias: float32 [2, 120], replicated, may hold values from -3 to 3
Outputs:
- restored: bfloat16 [8, 120, 32, 128], P(('clips', 'tm'), None, 'tile'), parts along dimension 0
The draws below stay inside these ranges and needn't reach their ends.
There are 2 independent parts, one for each index of `clips`. The reference program is written for one: setup_inputs(seed, part) draws one part's arguments, and reference() takes and returns one part's arrays. A program takes and returns all parts, laid end to end along the dimension named above; an argument that names none is the same for every part. Nothing has to cross between parts.
All inputs are finite; a program needn't handle non-finite values.
Results may differ from the reference program's by a relative error of at most 0.0084.
Values may be sent and summed in bfloat16 or wider, within the bound.
No kernel may reach another device: no remote copies, remote signals or barrier semaphores. Data moves between devices by JAX's collectives and lax.ppermute only.
A program may use at most 64 MiB of HBM per device.

```python
import jax
import jax.numpy as jnp
from jax import lax

HEADS = 6
HD = 20
C = 120
FF = 240
LAYERS = 2
W = 128
FRAMES = 4
H = 32


def draw_qkv_weight(key, part):
    base = jax.random.normal(key, (LAYERS, C, 3 * C), jnp.float32) * C ** (-0.5)
    return jnp.clip(base, -4.0, 4.0).astype(jnp.bfloat16)


def shard_levels(key, extent, cuts, smallest, largest):
    loudness = 1.0
    for axis_at, shards_of in cuts:
        draws = jax.random.uniform(jax.random.fold_in(jax.random.fold_in(key, 6), axis_at), (shards_of,), jnp.float32, smallest / len(cuts), largest / len(cuts))
        loudness = loudness * jnp.repeat(jnp.exp(draws), extent[axis_at] // shards_of).reshape((-1,) + (1,) * (len(extent) - 1 - axis_at))
    return loudness


def bell_draw(key, shape, width, limit, cuts=(), kind=jnp.bfloat16):
    factor_of = shard_levels(key, shape, cuts, -0.22, 0.18) if cuts else 1.0
    array = jax.random.normal(key, shape, jnp.float32) * width * factor_of
    return jnp.minimum(jnp.maximum(array, -limit), limit).astype(kind)


def setup_inputs(seed: int = 0, part: int = 0) -> dict:
    key_list = jax.random.split(jax.random.key(seed), 10)
    part_keys = jax.random.split(jax.random.fold_in(key_list[9], part), 10)
    frames = bell_draw(part_keys[0], (FRAMES, C, H, W), 1.0, 6.0, ((0, 4), (2, 4)))
    ln_gain = jnp.clip(jax.random.uniform(key_list[1], (LAYERS, 2, C), jnp.float32, 0.5, 1.5), 0.5, 1.5)
    qkv_weight = draw_qkv_weight(jax.random.fold_in(key_list[9], 71), part)
    out_weight = bell_draw(key_list[3], (LAYERS, C, C), C ** -0.5, 0.5)
    gate_weight = bell_draw(key_list[4], (LAYERS, C, FF), C ** -0.5, 0.5)
    up_weight = bell_draw(key_list[5], (LAYERS, C, FF), C ** -0.5, 0.5)
    down_weight = bell_draw(key_list[6], (LAYERS, FF, C), FF ** -0.5, 0.375)
    conv_weight = bell_draw(key_list[7], (LAYERS, 9, C, C), (9 * C) ** -0.5, 0.1875)
    conv_bias = bell_draw(key_list[8], (LAYERS, C), 0.5, 3.0, (), jnp.float32)
    return {"frames": frames, "ln_gain": ln_gain, "qkv_weight": qkv_weight, "out_weight": out_weight, "gate_weight": gate_weight, "up_weight": up_weight, "down_weight": down_weight, "conv_weight": conv_weight, "conv_bias": conv_bias}


def layer_norm(tensor, gain):
    center = tensor - lax.optimization_barrier(jnp.mean(tensor, axis=-3, keepdims=True))
    spread = lax.optimization_barrier(jnp.mean(center * center, axis=-3, keepdims=True))
    return (center * lax.rsqrt(spread + 1e-05) * gain[:, None, None]).astype(jnp.bfloat16)

def to_windows(tensor):
    row_count, col_count = (tensor.shape[1], tensor.shape[2])
    split = tensor.reshape(HEADS, HD, row_count // 8, 8, col_count // 8, 8)
    return split.transpose(0, 2, 4, 3, 5, 1).reshape(HEADS, row_count // 8 * (col_count // 8), 64, HD)

def from_windows(tensor, row_count, col_count):
    split = tensor.reshape(HEADS, row_count // 8, col_count // 8, 8, 8, HD)
    return split.transpose(0, 5, 1, 3, 2, 4).reshape(HEADS * HD, row_count, col_count)

def attention(queries, own_keys, own_values, far_keys, far_values):
    row_count, col_count = (queries.shape[1], queries.shape[2])
    q_windows = to_windows(queries).astype(jnp.float32)
    all_keys = jnp.concatenate([to_windows(own_keys), to_windows(far_keys)], axis=2).astype(jnp.float32)
    all_values = jnp.concatenate([to_windows(own_values), to_windows(far_values)], axis=2).astype(jnp.float32)
    scores = jnp.einsum('hnqd,hnkd->hnqk', q_windows, all_keys) * HD ** (-0.5)
    weights = lax.optimization_barrier(jax.nn.softmax(scores, axis=-1).astype(jnp.bfloat16)).astype(jnp.float32)
    result = jnp.einsum('hnqk,hnkd->hnqd', weights, all_values)
    return from_windows(result, row_count, col_count).astype(jnp.bfloat16)

def project(tensor, weight):
    return jnp.einsum('crw,cd->drw', tensor.astype(jnp.float32), weight.astype(jnp.float32))

def reference(frames, ln_gain, qkv_weight, out_weight, gate_weight, up_weight, down_weight, conv_weight, conv_bias):
    stream = frames.astype(jnp.float32)
    frame_ids = jnp.arange(FRAMES, dtype=jnp.int32)
    for layer_index in range(LAYERS):
        shifted = layer_index % 2 == 1
        normed = layer_norm(stream, ln_gain[layer_index, 0])
        if shifted:
            window_input = jnp.roll(normed, (-4, -4), axis=(2, 3))
        else:
            window_input = normed
        packed = lax.map(lambda one_frame: project(one_frame, qkv_weight[layer_index]).astype(jnp.bfloat16), window_input)
        queries = packed[:, :C]
        key_all = packed[:, C:2 * C]
        value_all = packed[:, 2 * C:]
        if shifted:
            partner = jnp.where(frame_ids % 2 == 1, (frame_ids + 1) % FRAMES, (frame_ids - 1) % FRAMES).astype(jnp.int32)
        else:
            partner = jnp.bitwise_xor(frame_ids, 1).astype(jnp.int32)
        mixed = lax.map(lambda group: attention(*group), (queries, key_all, value_all, key_all[partner], value_all[partner]))
        if shifted:
            unrolled = jnp.roll(mixed, (4, 4), axis=(2, 3))
        else:
            unrolled = mixed
        attended = stream + lax.map(lambda one_frame: project(one_frame, out_weight[layer_index]), unrolled)
        normed_ff = layer_norm(attended, ln_gain[layer_index, 1])

        def feed(one_frame):
            gate_part = project(one_frame, gate_weight[layer_index])
            up_part = project(one_frame, up_weight[layer_index])
            hidden = (jax.nn.gelu(gate_part, approximate=False) * up_part).astype(jnp.bfloat16)
            return project(hidden, down_weight[layer_index])
        fed = attended + lax.map(feed, normed_ff)
        rounded = fed.astype(jnp.bfloat16)

        def convolve(one_frame):
            padded = jnp.pad(one_frame, ((0, 0), (1, 1), (1, 1)))
            row_count, col_count = (one_frame.shape[1], one_frame.shape[2])
            total = jnp.zeros((C, row_count, col_count), jnp.float32)
            for tap_row in range(3):
                for tap_col in range(3):
                    window = padded[:, tap_row:tap_row + row_count, tap_col:tap_col + col_count]
                    total = total + project(window, conv_weight[layer_index, 3 * tap_row + tap_col])
            return total
        stream = fed + lax.map(convolve, rounded) + conv_bias[layer_index][None, :, None, None]
    return stream.astype(jnp.bfloat16)
```

```python
import jax
import jax.numpy as jnp
from jax import lax
from jax.experimental import pallas as pl
from jax.experimental.pallas import tpu as pltpu
from jax.sharding import PartitionSpec as P

HEADS = 6
HD = 20
LAYERS = 2
WIN = 8
LANES = 128
BF = jnp.bfloat16
F32 = jnp.float32
NT = (((1,), (1,)), ((), ()))


def up(n):
    return -(-n // LANES) * LANES


def dot(a, b):
    return jnp.dot(a, b, preferred_element_type=F32)


def dot_nt(a, b):
    return lax.dot_general(a, b, NT, preferred_element_type=F32)


def norm(x, gain, channels):
    lane = lax.broadcasted_iota(jnp.int32, x.shape, x.ndim - 1)
    mean = jnp.sum(x, axis=-1, keepdims=True) * (1.0 / channels)
    center = jnp.where(lane < channels, x - mean, 0.0)
    spread = jnp.sum(center * center, axis=-1, keepdims=True) * (1.0 / channels)
    return center * lax.rsqrt(spread + 1e-05) * gain


def to_positions(ref):
    x = ref[0].astype(F32)
    channels, rows, cols = x.shape
    x = jnp.concatenate([x, jnp.zeros((LANES - channels, rows, cols), F32)], axis=0)
    x = jnp.swapaxes(x, 0, 1)
    return jnp.stack([x[r].T for r in range(rows)], axis=0)


def windows(x):
    rows, cols, lanes = x.shape
    x = x.reshape(rows, cols // WIN, WIN, lanes)
    return jnp.swapaxes(x, 0, 1).reshape(cols // WIN, rows * WIN, lanes)


def unwindows(x, rows):
    count, _, lanes = x.shape
    x = jnp.swapaxes(x.reshape(count, rows, WIN, lanes), 0, 1)
    return x.reshape(rows, count * WIN, lanes)


def pad2(x, rows, cols):
    x = x.astype(F32)
    if x.shape[1] < cols:
        x = jnp.concatenate([x, jnp.zeros((x.shape[0], cols - x.shape[1]), F32)], axis=1)
    if x.shape[0] < rows:
        x = jnp.concatenate([x, jnp.zeros((rows - x.shape[0], cols), F32)], axis=0)
    return x


def weights_body(gain, qkv, out, gate, upw, down, conv, bias, o_gain, o_qk, o_vt, o_out, o_gu, o_down, o_conv, o_bias):
    layers, channels, _ = out.shape
    hidden = gate.shape[2]
    hp = up(hidden)
    for l in range(layers):
        o_gain[l] = pad2(gain[l], 2, LANES)
        o_bias[l] = pad2(bias[l : l + 1], 1, LANES)
        w = qkv[l].astype(F32)
        o_qk[l, :, :LANES] = pad2(w[:, :channels], LANES, LANES).astype(BF)
        o_qk[l, :, LANES:] = pad2(w[:, channels : 2 * channels], LANES, LANES).astype(BF)
        o_vt[l] = pad2(w[:, 2 * channels :], LANES, LANES).T.astype(BF)
        o_out[l] = pad2(out[l], LANES, LANES).astype(BF)
        o_gu[l, :, :hp] = pad2(gate[l], LANES, hp).astype(BF)
        o_gu[l, :, hp:] = pad2(upw[l], LANES, hp).astype(BF)
        o_down[l] = pad2(down[l], hp, LANES).astype(BF)
        for tap in range(9):
            a, b = divmod(tap, 3)
            o_conv[l, a, b * LANES : (b + 1) * LANES, :] = pad2(conv[l, tap], LANES, LANES).astype(BF)


def own_body(channels, x_ref, gain, qk, o_x, o_xn, o_q, o_k):
    x = to_positions(x_ref)
    own_tail(channels, windows(x), gain, qk, o_x, o_xn, o_q, o_k)


def own_tail(channels, x, gain, qk, o_x, o_xn, o_q, o_k):
    o_x[...] = x
    xn = norm(x, gain[0:1], channels).astype(BF)
    o_xn[...] = xn
    count, size, _ = xn.shape
    both = dot(xn.reshape(count * size, LANES), qk[...]).astype(BF)
    o_q[...] = both[:, :LANES].reshape(count, size, LANES)
    o_k[...] = both[:, LANES:].reshape(count, size, LANES)


def mutual(channels, far, x_ref, xn_ref, q_ref, k_ref, gain, qk, vt, wo, wgu, wd, emit):
    fn = norm(far, gain[0:1], channels).astype(BF)
    count, size, _ = fn.shape
    hp = wd.shape[0]
    fk = dot(fn.reshape(count * size, LANES), qk[:, LANES:]).astype(BF).reshape(count, size, LANES)
    head_of = lax.broadcasted_iota(jnp.int32, (size, LANES), 1) // HD
    sub = lax.broadcasted_iota(jnp.int32, (LANES, LANES), 0) // HD
    half = lax.broadcasted_iota(jnp.int32, (LANES, LANES), 1) // size
    pick = [sub == 2 * j + half for j in range(HEADS // 2)]
    scale = HD ** (-0.5) * 1.4426950408889634
    group = 4
    for g in range(count // group):
        mixed = []
        for w in range(g * group, (g + 1) * group):
            keys = jnp.concatenate([k_ref[w], fk[w]], axis=0)
            xall = jnp.concatenate([xn_ref[w], fn[w]], axis=0)
            vals = dot_nt(vt[...], xall).astype(BF)
            q = q_ref[w]
            qm = jnp.concatenate([jnp.where(head_of == h, q, jnp.zeros_like(q)) for h in range(HEADS)], axis=0)
            s = dot_nt(keys, qm)
            top = jnp.max(s, axis=0, keepdims=True)
            p = jnp.exp2((s - top) * scale)
            p = (p * (1.0 / jnp.sum(p, axis=0, keepdims=True))).astype(BF)
            o = dot(vals, p)
            r = jnp.where(pick[0], o[:, :LANES], 0.0)
            for j in range(1, HEADS // 2):
                r = jnp.where(pick[j], o[:, j * LANES : (j + 1) * LANES], r)
            r = r.T
            mixed.append(r[:size] + r[size:])
        mixed = jnp.concatenate(mixed, axis=0).astype(BF)
        att = x_ref[g * group : (g + 1) * group].reshape(group * size, LANES) + dot(mixed, wo[...])
        nf = norm(att, gain[1:2], channels).astype(BF)
        gu = dot(nf, wgu[...])
        gate = gu[:, :hp]
        act = 0.5 * gate * (1.0 + lax.erf(gate * (0.5**0.5))) * gu[:, hp:]
        fed = att + dot(act.astype(BF), wd[...])
        emit(g * group, fed.reshape(group, size, LANES))


def conv_rows(x, shift, origin, drop, wc, bias):
    cols = x.shape[1]
    col = (lax.broadcasted_iota(jnp.int32, (cols, 1), 0) + origin) % cols
    rows = x.shape[0] - 2
    parts = []
    center = None
    for b in range(3):
        turn = (shift + 1 - b) % cols
        moved = pltpu.roll(x, turn, 1) if turn else x
        if b == 1:
            center = moved
        else:
            moved = jnp.where(col == (0 if b == 0 else cols - 1), 0.0, moved)
        parts.append(moved.astype(BF))
    cat = jnp.concatenate(parts, axis=2)
    total = center[1 : 1 + rows] + bias[...]
    total = total.reshape(rows * x.shape[1], LANES)
    for a in range(3):
        part = drop(a, cat[a : a + rows])
        total = total + dot(part.reshape(rows * x.shape[1], 3 * LANES), wc[a])
    return total.reshape(rows, x.shape[1], LANES)


def wrap_drop(last, edge):
    def drop(a, part):
        if a == 1:
            return part
        at = edge if a == 0 else edge - 1
        row = jnp.where(last, 0.0, part[at : at + 1].astype(F32)).astype(BF)
        return jnp.concatenate([part[:at], row, part[at + 1 :]], axis=0)

    return drop


def layer0_body(channels, far_ref, x_ref, xn_ref, q_ref, k_ref, gain, qk, vt, wo, wgu, wd, o_fed, o_low, o_high, buf):
    far = windows(to_positions(far_ref))
    rows = buf.shape[0]
    keep = o_low.shape[0]

    def emit(at, fed):
        buf[:, at * WIN : (at + fed.shape[0]) * WIN, :] = unwindows(fed, rows)

    mutual(channels, far, x_ref, xn_ref, q_ref, k_ref, gain, qk, vt, wo, wgu, wd, emit)
    o_fed[...] = buf[rows - keep :]
    o_low[...] = buf[:keep].astype(BF)
    o_high[...] = buf[rows - keep :].astype(BF)


def shifted_stream(last, high, low, wc, bias):
    x = jnp.concatenate([high, low], axis=0)
    x = conv_rows(x, -(WIN // 2), WIN // 2, wrap_drop(last, WIN // 2), wc, bias)
    return windows(x)


def own1_body(channels, last_ref, high, low, wc, bias, gain, qk, o_x, o_xn, o_q, o_k):
    x = shifted_stream(last_ref[0] == 1, high[...], low[...].astype(F32), wc, bias)
    own_tail(channels, x, gain, qk, o_x, o_xn, o_q, o_k)


def layer1_body(channels, last_ref, high, low, x_ref, xn_ref, q_ref, k_ref, wc, bias, gain, qk, vt, wo, wgu, wd, o_fed, o_send, buf):
    far = shifted_stream(last_ref[0] == 1, high[...].astype(F32), low[...].astype(F32), wc, bias)
    rows = buf.shape[0]
    keep = o_send.shape[0]

    def emit(at, fed):
        buf[:, at * WIN : (at + fed.shape[0]) * WIN, :] = unwindows(fed, rows)

    mutual(channels, far, x_ref, xn_ref, q_ref, k_ref, gain, qk, vt, wo, wgu, wd, emit)
    o_fed[...] = buf[:keep]
    o_send[...] = buf[rows - keep :].astype(BF)


def final_body(channels, last_ref, high, own, wc, bias, o_ref):
    first, last = last_ref[1] == 1, last_ref[0] == 1
    high = high[...].astype(F32)
    own = own[...]
    top = jnp.where(first, 0.0, high[:1])
    low = jnp.where(last, 0.0, own[-1:])
    x = jnp.concatenate([top, high[1:], own[:-1], low], axis=0)
    y = conv_rows(x, WIN // 2, 0, lambda a, part: part, wc, bias)
    y = jnp.stack([y[r].T for r in range(y.shape[0])], axis=0)
    y = jnp.swapaxes(y, 0, 1)[:channels]
    o_ref[0] = y.astype(BF)


def call(body, outs, *args, scratch=(), scalars=0):
    vm = pl.BlockSpec(memory_space=pltpu.VMEM)
    sm = pl.BlockSpec(memory_space=pltpu.SMEM)
    return pl.pallas_call(
        body,
        out_shape=[jax.ShapeDtypeStruct(s, d) for s, d in outs],
        in_specs=[sm] * scalars + [vm] * (len(args) - scalars),
        out_specs=[vm] * len(outs),
        scratch_shapes=list(scratch),
        compiler_params=pltpu.CompilerParams(vmem_limit_bytes=24 * 1024 * 1024),
    )(*args)


def on_device(frames, ln_gain, qkv_weight, out_weight, gate_weight, up_weight, down_weight, conv_weight, conv_bias):
    _, channels, rows, cols = frames.shape
    layers = ln_gain.shape[0]
    hp = up(gate_weight.shape[2])
    tiles, depth = lax.axis_size("tile"), lax.axis_size("tm")
    where = lax.axis_index("tile")
    ends = jnp.stack([where == tiles - 1, where == 0]).astype(jnp.int32)
    axes = ("tile", "tm")

    def odd(f):
        return (f + 1) % depth if f % 2 else (f - 1) % depth

    def send(x, target):
        pairs = []
        for t in range(tiles):
            for f in range(depth):
                to_t, to_f = target(t, f)
                pairs.append((t * depth + f, to_t * depth + to_f))
        return lax.ppermute(x, axes, pairs)

    far_frames = send(frames, lambda t, f: (t, f ^ 1))
    gain, qk, vt, wo, wgu, wd, wc, bias = call(
        weights_body,
        [
            ((layers, 2, LANES), F32),
            ((layers, LANES, 2 * LANES), BF),
            ((layers, LANES, LANES), BF),
            ((layers, LANES, LANES), BF),
            ((layers, LANES, 2 * hp), BF),
            ((layers, hp, LANES), BF),
            ((layers, 3, 3 * LANES, LANES), BF),
            ((layers, 1, LANES), F32),
        ],
        ln_gain, qkv_weight, out_weight, gate_weight, up_weight, down_weight, conv_weight, conv_bias,
    )
    count = cols // WIN
    own_outs = [
        ((count, rows * WIN, LANES), F32),
        ((count, rows * WIN, LANES), BF),
        ((count, rows * WIN, LANES), BF),
        ((count, rows * WIN, LANES), BF),
    ]
    half = (rows // 2 + 1, cols, LANES)
    buf = pltpu.VMEM((rows, cols, LANES), F32)

    def bind(body):
        def wrapped(*refs):
            return body(channels, *refs)
        wrapped.__name__ = body.__name__
        return wrapped

    x, xn, q, k = call(bind(own_body), own_outs, frames, gain[0], qk[0])
    fed, low, high = call(
        bind(layer0_body),
        [(half, F32), (half, BF), (half, BF)],
        far_frames, x, xn, q, k, gain[0], qk[0], vt[0], wo[0], wgu[0], wd[0],
        scratch=[buf],
    )
    below = send(low, lambda t, f: ((t - 1) % tiles, f))
    far_high = send(high, lambda t, f: (t, odd(f)))
    far_low = send(low, lambda t, f: ((t - 1) % tiles, odd(f)))
    x, xn, q, k = call(bind(own1_body), own_outs, ends, fed, below, wc[0], bias[0], gain[1], qk[1], scalars=1)
    fed, down = call(
        bind(layer1_body),
        [(half, F32), (half, BF)],
        ends, far_high, far_low, x, xn, q, k, wc[0], bias[0], gain[1], qk[1], vt[1], wo[1], wgu[1], wd[1],
        scratch=[buf], scalars=1,
    )
    above = send(down, lambda t, f: ((t + 1) % tiles, f))
    (out,) = call(bind(final_body), [((1, channels, rows, cols), BF)], ends, above, fed, wc[1], bias[1], scalars=1)
    return out


def solution(mesh):
    in_specs = (P(("clips", "tm"), None, "tile", None), P(), P(), P(), P(), P(), P(), P(), P())
    out_specs = P(("clips", "tm"), None, "tile", None)
    return jax.shard_map(
        on_device, mesh=mesh, in_specs=in_specs, out_specs=out_specs, check_vma=False
    )
```

```python
import jax
import jax.numpy as jnp
from jax import lax
from jax.experimental import pallas as pl
from jax.experimental.pallas import tpu as pltpu
from jax.sharding import PartitionSpec as P


HEADS = 6
HD = 20
WIN = 8
LANES = 128
GROUP = 4
BF = jnp.bfloat16
F32 = jnp.float32
NT = (((1,), (1,)), ((), ()))


def up(n):
    return -(-n // LANES) * LANES


def dot(a, b):
    return jnp.dot(a, b, preferred_element_type=F32)


def dot_nt(a, b):
    return lax.dot_general(a, b, NT, preferred_element_type=F32)


def norm(x, gain, channels):
    lane = lax.broadcasted_iota(jnp.int32, x.shape, x.ndim - 1)
    mean = jnp.sum(x, axis=-1, keepdims=True) * (1.0 / channels)
    center = jnp.where(lane < channels, x - mean, 0.0)
    spread = jnp.sum(center * center, axis=-1, keepdims=True) * (1.0 / channels)
    return center * lax.rsqrt(spread + 1e-05) * gain


def to_positions(ref):
    x = ref[0].astype(F32)
    channels, rows, cols = x.shape
    x = jnp.concatenate([x, jnp.zeros((LANES - channels, rows, cols), F32)], axis=0)
    x = jnp.swapaxes(x, 0, 1)
    return jnp.stack([x[r].T for r in range(rows)], axis=0)


def windows(x):
    rows, cols, lanes = x.shape
    x = x.reshape(rows, cols // WIN, WIN, lanes)
    return jnp.swapaxes(x, 0, 1).reshape(cols // WIN, rows * WIN, lanes)


def unwindows(x, rows):
    count, _, lanes = x.shape
    x = jnp.swapaxes(x.reshape(count, rows, WIN, lanes), 0, 1)
    return x.reshape(rows, count * WIN, lanes)


def pad2(x, rows, cols):
    x = x.astype(F32)
    if x.shape[1] < cols:
        x = jnp.concatenate([x, jnp.zeros((x.shape[0], cols - x.shape[1]), F32)], axis=1)
    if x.shape[0] < rows:
        x = jnp.concatenate([x, jnp.zeros((rows - x.shape[0], cols), F32)], axis=0)
    return x


def norm_body(channels, gain_hbm, x_hbm, o_x, o_a, o_b, gain, x_ref, sems):
    copies = [pltpu.make_async_copy(x_hbm, x_ref, sems.at[0]), pltpu.make_async_copy(gain_hbm, gain, sems.at[1])]
    for copy in copies:
        copy.start()
    for copy in copies:
        copy.wait()
    x = windows(to_positions(x_ref))
    o_x[...] = x
    xn = norm(x, pad2(gain[0], 2, LANES)[:1], channels).astype(BF)
    first = o_a.shape[0]
    o_a[...] = xn[:first]
    o_b[...] = xn[first:]


def weights_body(channels, *refs):
    hbm, (xa, xb) = refs[:8], refs[8:10]
    o_q, o_k = refs[10:12]
    layers = hbm[2].shape[0]
    outs = refs[12 : 12 + 8 * layers]
    local, sems = refs[12 + 8 * layers : -1], refs[-1]
    copies = [pltpu.make_async_copy(a, b, sems.at[i]) for i, (a, b) in enumerate(zip(hbm, local))]
    for copy in copies:
        copy.start()
    for copy in copies:
        copy.wait()
    gain, qkv, out, gate, upw, down, conv, bias = local
    hp = up(gate.shape[2])
    for l in range(layers):
        o_gain, o_qk, o_vt, o_out, o_gu, o_down, o_conv, o_bias = outs[8 * l : 8 * l + 8]
        o_gain[...] = pad2(gain[l], 2, LANES)
        o_bias[...] = pad2(bias[l : l + 1], 1, LANES)
        w = qkv[l].astype(F32)
        wq = pad2(w[:, :channels], LANES, LANES).astype(BF)
        wk = pad2(w[:, channels : 2 * channels], LANES, LANES).astype(BF)
        o_qk[:, :LANES] = wq
        o_qk[:, LANES:] = wk
        o_vt[...] = pad2(w[:, 2 * channels :], LANES, LANES).T.astype(BF)
        o_out[...] = pad2(out[l], LANES, LANES).astype(BF)
        o_gu[:, :hp] = pad2(gate[l], LANES, hp).astype(BF)
        o_gu[:, hp:] = pad2(upw[l], LANES, hp).astype(BF)
        o_down[...] = pad2(down[l], hp, LANES).astype(BF)
        for tap in range(9):
            a, b = divmod(tap, 3)
            o_conv[a, b * LANES : (b + 1) * LANES, :] = pad2(conv[l, tap], LANES, LANES).astype(BF)
        if l == 0:
            project(jnp.concatenate([xa[...], xb[...]], axis=0), jnp.concatenate([wq, wk], axis=1), o_q, o_k)


def project(xn, qk, o_q, o_k):
    count, size, _ = xn.shape
    both = dot(xn.reshape(count * size, LANES), qk).astype(BF)
    o_q[...] = both[:, :LANES].reshape(count, size, LANES)
    o_k[...] = both[:, LANES:].reshape(count, size, LANES)


def mutual(channels, base, fn, own, x_ref, q_ref, k_ref, gain, qk, vt, wo, wgu, wd, emit):
    count, size, _ = fn.shape
    hp = wd.shape[0]
    fk = dot(fn.reshape(count * size, LANES), qk[:, LANES:]).astype(BF).reshape(count, size, LANES)
    head_of = lax.broadcasted_iota(jnp.int32, (size, LANES), 1) // HD
    sub = lax.broadcasted_iota(jnp.int32, (LANES, LANES), 0) // HD
    half = lax.broadcasted_iota(jnp.int32, (LANES, LANES), 1) // size
    pick = [sub == 2 * j + half for j in range(HEADS // 2)]
    scale = HD ** (-0.5) * 1.4426950408889634
    group = next(g for g in range(min(GROUP, count), 0, -1) if count % g == 0)
    if group < 3:
        group = count

    def scores(g, _):
        out = []
        for w in range(g * group, (g + 1) * group):
            keys = jnp.concatenate([k_ref[base + w], fk[w]], axis=0)
            xall = jnp.concatenate([own[w], fn[w]], axis=0)
            vals = dot_nt(vt[...], xall).astype(BF)
            q = q_ref[base + w]
            qm = jnp.concatenate([jnp.where(head_of == h, q, jnp.zeros_like(q)) for h in range(HEADS)], axis=0)
            out.append((vals, dot_nt(keys, qm)))
        return out

    def attend(g, state):
        out = []
        for vals, s in state:
            top = jnp.max(s, axis=0, keepdims=True)
            p = jnp.exp2((s - top) * scale)
            p = (p * (1.0 / jnp.sum(p, axis=0, keepdims=True))).astype(BF)
            out.append(dot(vals, p))
        return out

    def merge(g, state):
        mixed = []
        for o in state:
            r = jnp.where(pick[0], o[:, :LANES], 0.0)
            for j in range(1, HEADS // 2):
                r = jnp.where(pick[j], o[:, j * LANES : (j + 1) * LANES], r)
            r = r.T
            mixed.append(r[:size] + r[size:])
        mixed = jnp.concatenate(mixed, axis=0).astype(BF)
        return x_ref[base + g * group : base + (g + 1) * group].reshape(group * size, LANES) + dot(mixed, wo[...])

    def widen(g, att):
        nf = norm(att, gain[1:2], channels).astype(BF)
        return att, dot(nf, wgu[...])

    def narrow(g, state):
        att, gu = state
        gate = gu[:, :hp]
        act = 0.5 * gate * (1.0 + lax.erf(gate * (0.5**0.5))) * gu[:, hp:]
        fed = att + dot(act.astype(BF), wd[...])
        emit(g * group, fed.reshape(group, size, LANES))

    stages = [scores, attend, merge, widen, narrow]
    total = count // group
    held = [None] * (len(stages) + 1)
    for step in range(total + len(stages) - 1):
        for i in reversed(range(len(stages))):
            if 0 <= step - i < total:
                held[i + 1] = stages[i](step - i, held[i])


def conv_rows(x, shift, origin, drop, wc, bias):
    cols = x.shape[1]
    taps = [pltpu.roll(x, (shift + 1 - b) % cols, 1) if (shift + 1 - b) % cols else x for b in range(3)]
    return conv_taps(taps, origin, cols, drop, wc, bias)


def conv_cols(x, skip, origin, cols, drop, wc, bias):
    n = x.shape[1] - 2 * skip
    taps = [x[:, skip - 1 + b : skip - 1 + b + n] for b in range(3)]
    return conv_taps(taps, origin, cols, drop, wc, bias)


def conv_taps(taps, origin, cols, drop, wc, bias):
    center = taps[1]
    rows, width = center.shape[0] - 2, center.shape[1]
    col = (lax.broadcasted_iota(jnp.int32, (width, 1), 0) + origin) % cols
    parts = []
    for b, moved in enumerate(taps):
        if b != 1:
            moved = jnp.where(col == (0 if b == 0 else cols - 1), 0.0, moved)
        parts.append(moved.astype(BF))
    cat = jnp.concatenate(parts, axis=2)
    total = (center[1 : 1 + rows] + bias[...]).reshape(rows * width, LANES)
    for a in range(3):
        part = drop(a, cat[a : a + rows])
        total = total + dot(part.reshape(rows * width, 3 * LANES), wc[a])
    return total.reshape(rows, width, LANES)


def wrap_drop(last, edge):
    def drop(a, part):
        if a == 1:
            return part
        at = edge if a == 0 else edge - 1
        row = jnp.where(last, 0.0, part[at : at + 1].astype(F32)).astype(BF)
        return jnp.concatenate([part[:at], row, part[at + 1 :]], axis=0)

    return drop


def collect(buf):
    def emit(at, fed):
        buf[:, at * WIN : (at + fed.shape[0]) * WIN, :] = unwindows(fed, buf.shape[0])

    return emit


def layer0_first(channels, far, own, x_ref, q_ref, k_ref, gain, qk, vt, wo, wgu, wd, o_fed, o_low, o_high, buf):
    rows, keep = buf.shape[0], o_low.shape[0]
    mutual(channels, 0, far[...], own[...], x_ref, q_ref, k_ref, gain, qk, vt, wo, wgu, wd, collect(buf))
    o_fed[...] = buf[rows - keep :]
    o_low[...] = buf[:keep].astype(BF)
    o_high[...] = buf[rows - keep :].astype(BF)


def layer0_second(channels, far, own, x_ref, q_ref, k_ref, gain, qk, vt, wo, wgu, wd, low_a, o_fed, o_low, o_high, o_whole, buf):
    rows, keep = buf.shape[0], o_low.shape[0]
    base = x_ref.shape[0] - far.shape[0]
    mutual(channels, base, far[...], own[...], x_ref, q_ref, k_ref, gain, qk, vt, wo, wgu, wd, collect(buf))
    o_fed[...] = buf[rows - keep :]
    low = buf[:keep].astype(BF)
    o_low[...] = low
    o_high[...] = buf[rows - keep :].astype(BF)
    first = base * WIN
    o_whole[:, :first, :] = low_a[...]
    o_whole[:, first:, :] = low


def own1_body(channels, ends, fed_a, fed_b, low, wc, bias, gain, qk, o_x, o_xn, o_q, o_k):
    high = jnp.concatenate([fed_a[...], fed_b[...]], axis=1)
    x = jnp.concatenate([high, low[...].astype(F32)], axis=0)
    x = windows(conv_rows(x, -(WIN // 2), WIN // 2, wrap_drop(ends[0] == 1, WIN // 2), wc, bias))
    o_x[...] = x
    xn = norm(x, gain[0:1], channels).astype(BF)
    o_xn[...] = xn
    project(xn, qk[...], o_q, o_k)


def far_normed(channels, ends, x, base, cols, wc, bias, gain):
    x = conv_cols(x, WIN // 2, base + WIN // 2, cols, wrap_drop(ends[0] == 1, WIN // 2), wc, bias)
    return norm(windows(x), gain[0:1], channels).astype(BF)


def layer1_first(channels, ends, high, low, xn_ref, x_ref, q_ref, k_ref, wc, bias, gain0, gain, qk, vt, wo, wgu, wd, o_own, o_send, buf):
    x = jnp.concatenate([high[...], low[...]], axis=0).astype(F32)
    rows, keep = buf.shape[0], o_own.shape[0]
    count = buf.shape[1] // WIN
    fn = far_normed(channels, ends, x, 0, 2 * buf.shape[1], wc, bias, gain)
    mutual(channels, 0, fn, xn_ref[:count], x_ref, q_ref, k_ref, gain, qk, vt, wo, wgu, wd, collect(buf))
    o_own[...] = buf[:keep]
    o_send[...] = buf[rows - keep :].astype(BF)


def layer1_second(channels, ends, high_a, low_a, high_b, low_b, xn_ref, x_ref, q_ref, k_ref, wc, bias, gain0, gain, qk, vt, wo, wgu, wd, send_a, o_own, o_send, buf):
    xa = jnp.concatenate([high_a[...], low_a[...]], axis=0).astype(F32)
    xb = jnp.concatenate([high_b[...], low_b[...]], axis=0).astype(F32)
    half = buf.shape[1]
    x = jnp.concatenate([xa[:, half:], xb, xa[:, :WIN]], axis=1)
    rows, keep = buf.shape[0], o_own.shape[0]
    count = half // WIN
    fn = far_normed(channels, ends, x, half, 2 * half, wc, bias, gain)
    mutual(channels, count, fn, xn_ref[count:], x_ref, q_ref, k_ref, gain, qk, vt, wo, wgu, wd, collect(buf))
    o_own[...] = buf[:keep]
    o_send[:, :half, :] = send_a[...]
    o_send[:, half:, :] = buf[rows - keep :].astype(BF)


def final_body(channels, ends, high, own_a, own_b, wc, bias, o_ref):
    first, last = ends[1] == 1, ends[0] == 1
    high = high[...].astype(F32)
    own = jnp.concatenate([own_a[...], own_b[...]], axis=1)
    top = jnp.where(first, 0.0, high[:1])
    low = jnp.where(last, 0.0, own[-1:])
    x = jnp.concatenate([top, high[1:], own[:-1], low], axis=0)
    y = conv_rows(x, WIN // 2, 0, lambda a, part: part, wc, bias)
    y = jnp.stack([y[r].T for r in range(y.shape[0])], axis=0)
    y = jnp.swapaxes(y, 0, 1)[:channels]
    o_ref[0] = y.astype(BF)


def call(body, outs, *args, scratch=(), scalars=0, remote=0, work=0):
    vm = pl.BlockSpec(memory_space=pltpu.VMEM)
    sm = pl.BlockSpec(memory_space=pltpu.SMEM)
    hbm = pl.BlockSpec(memory_space=pltpu.HBM)
    specs = [sm] * scalars + [hbm] * remote
    cost = pl.CostEstimate(flops=work, bytes_accessed=1024, transcendentals=0) if work else None
    run = pl.pallas_call(
        body,
        out_shape=[jax.ShapeDtypeStruct(s, d) for s, d in outs],
        in_specs=specs + [vm] * (len(args) - len(specs)),
        out_specs=[vm] * len(outs),
        scratch_shapes=list(scratch),
        cost_estimate=cost,
        compiler_params=pltpu.CompilerParams(vmem_limit_bytes=24 * 1024 * 1024),
    )
    args = [pltpu.with_memory_space_constraint(a, pltpu.HBM) if i < scalars + remote and i >= scalars else a for i, a in enumerate(args)]
    return run(*args)


def section(frames, *params):
    ln_gain, gate_weight = params[0], params[3]
    _, channels, rows, cols = frames.shape
    layers = ln_gain.shape[0]
    hp = up(gate_weight.shape[2])
    tiles, depth = lax.axis_size("tile"), lax.axis_size("tm")
    where = lax.axis_index("tile")
    ends = jnp.stack([where == tiles - 1, where == 0]).astype(jnp.int32)
    axes = ("tile", "tm")

    def odd(f):
        return (f + 1) % depth if f % 2 else (f - 1) % depth

    def send(x, target):
        pairs = []
        for t in range(tiles):
            for f in range(depth):
                to_t, to_f = target(t, f)
                pairs.append((t * depth + f, to_t * depth + to_f))
        return lax.ppermute(x, axes, pairs)

    def bind(body):
        def wrapped(*refs):
            return body(channels, *refs)

        wrapped.__name__ = body.__name__
        return wrapped

    count = cols // WIN
    first = count // 2 + 1
    rest = count - first
    keep = rows // 2 + 1
    size = rows * WIN
    dma = pltpu.SemaphoreType.DMA
    x, xa, xb = call(bind(norm_body),
        [((count, size, LANES), F32), ((first, size, LANES), BF), ((rest, size, LANES), BF)],
        ln_gain, frames,
        scratch=[pltpu.VMEM(ln_gain.shape, F32), pltpu.VMEM(frames.shape, BF), dma((2,))],
        remote=2,
    )
    far_a = send(xa, lambda t, f: (t, f ^ 1))
    far_b = send(xb, lambda t, f: (t, f ^ 1))
    q, k, *sets = call(bind(weights_body),
        [((count, size, LANES), BF), ((count, size, LANES), BF)]
        + [
            ((2, LANES), F32),
            ((LANES, 2 * LANES), BF),
            ((LANES, LANES), BF),
            ((LANES, LANES), BF),
            ((LANES, 2 * hp), BF),
            ((hp, LANES), BF),
            ((3, 3 * LANES, LANES), BF),
            ((1, LANES), F32),
        ]
        * layers,
        *params, xa, xb,
        scratch=[pltpu.VMEM(p.shape, p.dtype) for p in params] + [dma((len(params),))],
        remote=len(params),
    )

    gain, qk, vt, wo, wgu, wd, wc, bias = zip(*[sets[8 * l : 8 * l + 8] for l in range(layers)])

    def buf(n):
        return pltpu.VMEM((rows, n * WIN, LANES), F32)

    def piece(n, dtype=BF):
        return ((keep, n * WIN, LANES), dtype)

    inner = (gain[0], qk[0], vt[0], wo[0], wgu[0], wd[0])
    fed_a, low_a, high_a = call(bind(layer0_first), [piece(first, F32), piece(first), piece(first)],
        far_a, xa, x, q, k, *inner, scratch=[buf(first)],
    )
    far_high_a = send(high_a, lambda t, f: (t, odd(f)))
    far_low_a = send(low_a, lambda t, f: ((t - 1) % tiles, odd(f)))
    fed_b, low_b, high_b, low = call(bind(layer0_second), [piece(rest, F32), piece(rest), piece(rest), piece(count)],
        far_b, xb, x, q, k, *inner, low_a, scratch=[buf(rest)],
    )
    below = send(low, lambda t, f: ((t - 1) % tiles, f))
    far_high_b = send(high_b, lambda t, f: (t, odd(f)))
    far_low_b = send(low_b, lambda t, f: ((t - 1) % tiles, odd(f)))
    whole = (count, size, LANES)
    x, xn, q, k = call(bind(own1_body), [(whole, F32), (whole, BF), (whole, BF), (whole, BF)],
        ends, fed_a, fed_b, below, wc[0], bias[0], gain[1], qk[1], scalars=1,
    )
    inner = (wc[0], bias[0], gain[0], gain[1], qk[1], vt[1], wo[1], wgu[1], wd[1])
    half = count // 2
    own_a, send_a = call(bind(layer1_first), [piece(half, F32), piece(half)],
        ends, far_high_a, far_low_a, xn, x, q, k, *inner, scratch=[buf(half)], scalars=1,
    )
    own_b, down = call(bind(layer1_second), [piece(half, F32), piece(count)],
        ends, far_high_a, far_low_a, far_high_b, far_low_b, xn, x, q, k, *inner, send_a, scratch=[buf(half)], scalars=1,
    )
    above = send(down, lambda t, f: ((t + 1) % tiles, f))
    (out,) = call(bind(final_body), [((1, channels, rows, cols), BF)], ends, above, own_a, own_b, wc[1], bias[1], scalars=1)
    return out


def solution(mesh):
    in_specs = (P(("clips", "tm"), None, "tile", None), P(), P(), P(), P(), P(), P(), P(), P())
    out_specs = P(("clips", "tm"), None, "tile", None)
    return jax.shard_map(section, mesh=mesh, in_specs=in_specs, out_specs=out_specs, check_vma=False)
```

```python
import jax
import jax.numpy as jnp
from jax import lax
from jax.experimental import pallas as pl
from jax.experimental.pallas import tpu as pltpu
from jax.sharding import PartitionSpec as P


HEADS = 6
HD = 20
WIN = 8
LANES = 128
GROUP = 8
BF = jnp.bfloat16
F32 = jnp.float32
NT = (((1,), (1,)), ((), ()))


def up(n):
    return -(-n // LANES) * LANES


def dot(a, b):
    return jnp.dot(a, b, preferred_element_type=F32)


def dot_nt(a, b):
    return lax.dot_general(a, b, NT, preferred_element_type=F32)


def norm(x, gain, channels):
    lane = lax.broadcasted_iota(jnp.int32, x.shape, x.ndim - 1)
    mean = jnp.sum(x, axis=-1, keepdims=True) * (1.0 / channels)
    center = jnp.where(lane < channels, x - mean, 0.0)
    spread = jnp.sum(center * center, axis=-1, keepdims=True) * (1.0 / channels)
    return center * lax.rsqrt(spread + 1e-05) * gain


def to_positions(ref):
    x = ref[0].astype(F32)
    channels, rows, cols = x.shape
    x = jnp.concatenate([x, jnp.zeros((LANES - channels, rows, cols), F32)], axis=0)
    x = jnp.swapaxes(x, 0, 1)
    return jnp.stack([x[r].T for r in range(rows)], axis=0)


def windows(x):
    rows, cols, lanes = x.shape
    x = x.reshape(rows, cols // WIN, WIN, lanes)
    return jnp.swapaxes(x, 0, 1).reshape(cols // WIN, rows * WIN, lanes)


def unwindows(x, rows):
    count, _, lanes = x.shape
    x = jnp.swapaxes(x.reshape(count, rows, WIN, lanes), 0, 1)
    return x.reshape(rows, count * WIN, lanes)


def pad2(x, rows, cols):
    x = x.astype(F32)
    if x.shape[1] < cols:
        x = jnp.concatenate([x, jnp.zeros((x.shape[0], cols - x.shape[1]), F32)], axis=1)
    if x.shape[0] < rows:
        x = jnp.concatenate([x, jnp.zeros((rows - x.shape[0], cols), F32)], axis=0)
    return x


def norm_body(channels, gain_hbm, x_hbm, o_x, *refs):
    o_parts, (gain, x_ref, sems) = refs[:-3], refs[-3:]
    copies = [pltpu.make_async_copy(x_hbm, x_ref, sems.at[0]), pltpu.make_async_copy(gain_hbm, gain, sems.at[1])]
    for copy in copies:
        copy.start()
    for copy in copies:
        copy.wait()
    x = windows(to_positions(x_ref))
    o_x[...] = x
    xn = norm(x, pad2(gain[0], 2, LANES)[:1], channels).astype(BF)
    at = 0
    for part in o_parts:
        part[...] = xn[at : at + part.shape[0]]
        at += part.shape[0]


def weights_body(channels, *refs):
    hbm, layers = refs[:8], refs[2].shape[0]
    local, sems = refs[-9:-1], refs[-1]
    xs, (o_q, o_k), outs = refs[8 : -11 - 8 * layers], refs[-11 - 8 * layers : -9 - 8 * layers], refs[-9 - 8 * layers : -9]
    copies = [pltpu.make_async_copy(a, b, sems.at[i]) for i, (a, b) in enumerate(zip(hbm, local))]
    for copy in copies:
        copy.start()
    for copy in copies:
        copy.wait()
    gain, qkv, out, gate, upw, down, conv, bias = local
    hp = up(gate.shape[2])
    for l in range(layers):
        o_gain, o_qk, o_vt, o_out, o_gu, o_down, o_conv, o_bias = outs[8 * l : 8 * l + 8]
        o_gain[...] = pad2(gain[l], 2, LANES)
        o_bias[...] = pad2(bias[l : l + 1], 1, LANES)
        w = qkv[l].astype(F32)
        wq = pad2(w[:, :channels], LANES, LANES).astype(BF)
        wk = pad2(w[:, channels : 2 * channels], LANES, LANES).astype(BF)
        o_qk[:, :LANES] = wq
        o_qk[:, LANES:] = wk
        o_vt[...] = pad2(w[:, 2 * channels :], LANES, LANES).T.astype(BF)
        o_out[...] = pad2(out[l], LANES, LANES).astype(BF)
        o_gu[:, :hp] = pad2(gate[l], LANES, hp).astype(BF)
        o_gu[:, hp:] = pad2(upw[l], LANES, hp).astype(BF)
        o_down[...] = pad2(down[l], hp, LANES).astype(BF)
        blank = jnp.zeros((3 * LANES, LANES), BF)
        o_conv[3 * 3 * LANES :, :LANES] = blank
        o_conv[: 3 * LANES, LANES:] = blank
        for tap in range(9):
            a, b = divmod(tap, 3)
            piece = pad2(conv[l, tap], LANES, LANES).astype(BF)
            for v in range(2):
                at = ((a + v) * 3 + b) * LANES
                o_conv[at : at + LANES, v * LANES : (v + 1) * LANES] = piece
        if l == 0:
            project(jnp.concatenate([part[...] for part in xs], axis=0), jnp.concatenate([wq, wk], axis=1), o_q, o_k)


def project(xn, qk, o_q, o_k):
    count, size, _ = xn.shape
    both = dot(xn.reshape(count * size, LANES), qk).astype(BF)
    o_q[...] = both[:, :LANES].reshape(count, size, LANES)
    o_k[...] = both[:, LANES:].reshape(count, size, LANES)


def pieces(count):
    n = -(-count // GROUP)
    edges = [count * i // n for i in range(n + 1)]
    return [(a, b - a) for a, b in zip(edges, edges[1:])]


def pipeline(stages, total):
    held = [None] * (len(stages) + 1)
    for step in range(total + len(stages) - 1):
        for i in reversed(range(len(stages))):
            if 0 <= step - i < total:
                held[i + 1] = stages[i](step - i, held[i])


def mutual(channels, base, count, far, own, x_ref, q_ref, k_ref, gain, qk, vt, wo, wgu, wd, emit):
    size = x_ref.shape[1]
    hp = wd.shape[0]
    head_of = lax.broadcasted_iota(jnp.int32, (size, LANES), 1) // HD
    sub = lax.broadcasted_iota(jnp.int32, (LANES, LANES), 0) // HD
    half = lax.broadcasted_iota(jnp.int32, (LANES, LANES), 1) // size
    pick = [sub == 2 * j + half for j in range(HEADS // 2)]
    scale = HD ** (-0.5) * 1.4426950408889634
    cuts = pieces(count)

    def fetch(g, _):
        at, n = cuts[g]
        fn = far(at, n)
        return fn, dot(fn.reshape(n * size, LANES), qk[:, LANES:]).astype(BF).reshape(n, size, LANES)

    def scores(g, state):
        fn, fk = state
        at, n = cuts[g]
        out = []
        for i in range(n):
            w = at + i
            keys = jnp.concatenate([k_ref[base + w], fk[i]], axis=0)
            xall = jnp.concatenate([own[w], fn[i]], axis=0)
            vals = dot_nt(vt[...], xall).astype(BF)
            q = q_ref[base + w]
            qm = jnp.concatenate([jnp.where(head_of == h, q, jnp.zeros_like(q)) for h in range(HEADS)], axis=0)
            out.append((vals, dot_nt(keys, qm)))
        return out

    def attend(g, state):
        out = []
        for vals, s in state:
            top = jnp.max(s, axis=0, keepdims=True)
            p = jnp.exp2((s - top) * scale)
            p = (p * (1.0 / jnp.sum(p, axis=0, keepdims=True))).astype(BF)
            out.append(dot(vals, p))
        return out

    def merge(g, state):
        mixed = []
        for o in state:
            r = jnp.where(pick[0], o[:, :LANES], 0.0)
            for j in range(1, HEADS // 2):
                r = jnp.where(pick[j], o[:, j * LANES : (j + 1) * LANES], r)
            r = r.T
            mixed.append(r[:size] + r[size:])
        mixed = jnp.concatenate(mixed, axis=0).astype(BF)
        at, n = cuts[g]
        return x_ref[base + at : base + at + n].reshape(n * size, LANES) + dot(mixed, wo[...])

    def widen(g, att):
        nf = norm(att, gain[1:2], channels).astype(BF)
        return att, dot(nf, wgu[...])

    def narrow(g, state):
        att, gu = state
        gate = gu[:, :hp]
        act = 0.5 * gate * (1.0 + lax.erf(gate * (0.5**0.5))) * gu[:, hp:]
        fed = att + dot(act.astype(BF), wd[...])
        at, n = cuts[g]
        emit(at, fed.reshape(n, size, LANES))

    pipeline([fetch, scores, attend, merge, widen, narrow], len(cuts))


def conv_rows(x, shift, origin, edge, wc, bias):
    cols = x.shape[1]
    taps = [pltpu.roll(x, (shift + 1 - b) % cols, 1) if (shift + 1 - b) % cols else x for b in range(3)]
    return conv_taps(taps, origin, cols, edge, wc, bias)


def conv_cols(x, skip, origin, cols, edge, wc, bias):
    n = x.shape[1] - 2 * skip
    taps = [x[:, skip - 1 + b : skip - 1 + b + n] for b in range(3)]
    return conv_taps(taps, origin, cols, edge, wc, bias)


def conv_taps(taps, origin, cols, edge, wc, bias):
    center = taps[1]
    rows, width = center.shape[0] - 2, center.shape[1]
    col = (lax.broadcasted_iota(jnp.int32, (width, 1), 0) + origin) % cols
    parts = []
    for b, moved in enumerate(taps):
        if b != 1:
            moved = jnp.where(col == (0 if b == 0 else cols - 1), 0.0, moved)
        parts.append(moved)
    lines = [jnp.concatenate([p[r] for p in parts], axis=1) for r in range(rows + 2)]
    packed = [line.astype(BF) for line in lines]
    blocks = []
    for j in range(rows // 2):
        four = packed[2 * j : 2 * j + 4]
        if edge is not None:
            last, at = edge
            if 2 * j + 1 == at - 1:
                four[3] = jnp.where(last, 0.0, lines[2 * j + 3]).astype(BF)
            if 2 * j == at:
                four[0] = jnp.where(last, 0.0, lines[2 * j]).astype(BF)
        blocks.append(jnp.concatenate(four, axis=1))
    mid = len(blocks) // 2
    both = [dot(jnp.concatenate(b, axis=0), wc[...]) for b in (blocks[:mid], blocks[mid:])]
    both = jnp.concatenate(both, axis=0)
    out = []
    for r in range(rows):
        j, v = divmod(r, 2)
        part = both[j * width : (j + 1) * width, v * LANES : (v + 1) * LANES]
        out.append(center[1 + r] + bias[...] + part)
    return jnp.stack(out, axis=0)


def collect(buf):
    def emit(at, fed):
        buf[:, at * WIN : (at + fed.shape[0]) * WIN, :] = unwindows(fed, buf.shape[0])

    return emit


def layer0_body(channels, base, far, own, x_ref, q_ref, k_ref, gain, qk, vt, wo, wgu, wd, *refs):
    buf = refs[-1]
    earlier = refs[: len(refs) - 4]
    outs = refs[len(earlier) : -1]
    rows, keep = buf.shape[0], outs[0].shape[0]
    mutual(channels, base, far.shape[0], lambda at, n: far[at : at + n], own, x_ref, q_ref, k_ref, gain, qk, vt, wo, wgu, wd, collect(buf))
    fresh = (buf[rows - keep :], buf[:keep].astype(BF), buf[rows - keep :].astype(BF))
    for out, now, old in zip(outs, fresh, earlier or (None,) * 3):
        edge = out.shape[1] - now.shape[1]
        if edge:
            out[:, :edge, :] = old[...]
        out[:, edge:, :] = now


def layer0_last(channels, base, far, own, x_ref, q_ref, k_ref, gain, qk, vt, wo, wgu, wd, low_a, o_fed, o_low, o_high, o_whole, buf):
    rows, keep = buf.shape[0], o_low.shape[0]
    mutual(channels, base, far.shape[0], lambda at, n: far[at : at + n], own, x_ref, q_ref, k_ref, gain, qk, vt, wo, wgu, wd, collect(buf))
    o_fed[...] = buf[rows - keep :]
    low = buf[:keep].astype(BF)
    o_low[...] = low
    o_high[...] = buf[rows - keep :].astype(BF)
    first = base * WIN
    o_whole[:, :first, :] = low_a[...]
    o_whole[:, first:, :] = low


def own1_body(channels, ends, fed_a, fed_b, low, wc, bias, gain, qk, o_x, o_xn, o_q, o_k):
    high = jnp.concatenate([fed_a[...], fed_b[...]], axis=1)
    x = jnp.concatenate([high, low[...].astype(F32)], axis=0)
    cols = x.shape[1]
    x = jnp.concatenate([x, x[:, :WIN]], axis=1)
    cuts = pieces(cols // WIN)

    def mix(g, _):
        at, n = cuts[g]
        part = x[:, at * WIN : (at + n + 1) * WIN]
        return windows(conv_cols(part, WIN // 2, at * WIN + WIN // 2, cols, (ends[0] == 1, WIN // 2), wc, bias))

    def finish(g, part):
        at, n = cuts[g]
        o_x[at : at + n] = part
        xn = norm(part, gain[0:1], channels).astype(BF)
        o_xn[at : at + n] = xn
        project(xn, qk[...], o_q.at[at : at + n], o_k.at[at : at + n])

    pipeline([mix, finish], len(cuts))


def far_normed(channels, ends, x, base, cols, wc, bias, gain):
    def far(at, n):
        part = x[:, at * WIN : (at + n + 1) * WIN]
        part = conv_cols(part, WIN // 2, base + at * WIN + WIN // 2, cols, (ends[0] == 1, WIN // 2), wc, bias)
        return norm(windows(part), gain[0:1], channels).astype(BF)

    return far


def layer1_first(channels, ends, high, low, xn_ref, x_ref, q_ref, k_ref, wc, bias, gain0, gain, qk, vt, wo, wgu, wd, o_own, o_send, buf):
    x = jnp.concatenate([high[...], low[...]], axis=0).astype(F32)
    rows, keep = buf.shape[0], o_own.shape[0]
    count = buf.shape[1] // WIN
    far = far_normed(channels, ends, x, 0, 2 * buf.shape[1], wc, bias, gain)
    mutual(channels, 0, count, far, xn_ref, x_ref, q_ref, k_ref, gain, qk, vt, wo, wgu, wd, collect(buf))
    o_own[...] = buf[:keep]
    o_send[...] = buf[rows - keep :].astype(BF)


def layer1_second(channels, ends, high_a, low_a, high_b, low_b, xn_ref, x_ref, q_ref, k_ref, wc, bias, gain0, gain, qk, vt, wo, wgu, wd, o_own, o_send, buf):
    xa = jnp.concatenate([high_a[...], low_a[...]], axis=0).astype(F32)
    xb = jnp.concatenate([high_b[...], low_b[...]], axis=0).astype(F32)
    half = buf.shape[1]
    x = jnp.concatenate([xa[:, half:], xb, xa[:, :WIN]], axis=1)
    rows, keep = buf.shape[0], o_own.shape[0]
    count = half // WIN
    far = far_normed(channels, ends, x, half, 2 * half, wc, bias, gain)
    mutual(channels, count, count, far, xn_ref.at[count:], x_ref, q_ref, k_ref, gain, qk, vt, wo, wgu, wd, collect(buf))
    o_own[...] = buf[:keep]
    o_send[...] = buf[rows - keep :].astype(BF)


def final_body(channels, ends, high_a, high_b, own_a, own_b, wc, bias, o_ref):
    first, last = ends[1] == 1, ends[0] == 1
    high = jnp.concatenate([high_a[...], high_b[...]], axis=1).astype(F32)
    own = jnp.concatenate([own_a[...], own_b[...]], axis=1)
    top = jnp.where(first, 0.0, high[:1])
    low = jnp.where(last, 0.0, own[-1:])
    x = jnp.concatenate([top, high[1:], own[:-1], low], axis=0)
    y = conv_rows(x, WIN // 2, 0, None, wc, bias)
    y = jnp.stack([y[r].T for r in range(y.shape[0])], axis=0)
    y = jnp.swapaxes(y, 0, 1)[:channels]
    o_ref[0] = y.astype(BF)


def call(body, outs, *args, scratch=(), scalars=0, remote=0, work=0):
    vm = pl.BlockSpec(memory_space=pltpu.VMEM)
    sm = pl.BlockSpec(memory_space=pltpu.SMEM)
    hbm = pl.BlockSpec(memory_space=pltpu.HBM)
    specs = [sm] * scalars + [hbm] * remote
    cost = pl.CostEstimate(flops=work, bytes_accessed=1024, transcendentals=0) if work else None
    run = pl.pallas_call(
        body,
        out_shape=[jax.ShapeDtypeStruct(s, d) for s, d in outs],
        in_specs=specs + [vm] * (len(args) - len(specs)),
        out_specs=[vm] * len(outs),
        scratch_shapes=list(scratch),
        cost_estimate=cost,
        compiler_params=pltpu.CompilerParams(vmem_limit_bytes=24 * 1024 * 1024),
    )
    args = [pltpu.with_memory_space_constraint(a, pltpu.HBM) if i < scalars + remote and i >= scalars else a for i, a in enumerate(args)]
    return run(*args)


def section(frames, *params):
    ln_gain, gate_weight = params[0], params[3]
    _, channels, rows, cols = frames.shape
    layers = ln_gain.shape[0]
    hp = up(gate_weight.shape[2])
    tiles, depth = lax.axis_size("tile"), lax.axis_size("tm")
    where = lax.axis_index("tile")
    ends = jnp.stack([where == tiles - 1, where == 0]).astype(jnp.int32)
    axes = ("tile", "tm")

    def odd(f):
        return (f + 1) % depth if f % 2 else (f - 1) % depth

    def send(x, target):
        pairs = []
        for t in range(tiles):
            for f in range(depth):
                to_t, to_f = target(t, f)
                pairs.append((t * depth + f, to_t * depth + to_f))
        return lax.ppermute(x, axes, pairs)

    def bind(body, *extra):
        def wrapped(*refs):
            return body(channels, *extra, *refs)

        wrapped.__name__ = body.__name__
        return wrapped

    count = cols // WIN
    first = count // 2 + 1
    rest = count - first
    keep = rows // 2 + 1
    size = rows * WIN
    dma = pltpu.SemaphoreType.DMA
    parts = [-(-first // 2), first // 2, rest]
    x, *xs = call(
        bind(norm_body),
        [((count, size, LANES), F32)] + [((n, size, LANES), BF) for n in parts],
        ln_gain, frames,
        scratch=[pltpu.VMEM(ln_gain.shape, F32), pltpu.VMEM(frames.shape, BF), dma((2,))],
        remote=2,
    )
    far = [send(part, lambda t, f: (t, f ^ 1)) for part in xs]
    q, k, *sets = call(bind(weights_body),
        [((count, size, LANES), BF), ((count, size, LANES), BF)]
        + [
            ((2, LANES), F32),
            ((LANES, 2 * LANES), BF),
            ((LANES, LANES), BF),
            ((LANES, LANES), BF),
            ((LANES, 2 * hp), BF),
            ((hp, LANES), BF),
            ((12 * LANES, 2 * LANES), BF),
            ((1, LANES), F32),
        ]
        * layers,
        *params, *xs,
        scratch=[pltpu.VMEM(p.shape, p.dtype) for p in params] + [dma((len(params),))],
        remote=len(params),
    )

    gain, qk, vt, wo, wgu, wd, wc, bias = zip(*[sets[8 * l : 8 * l + 8] for l in range(layers)])

    def buf(n):
        return pltpu.VMEM((rows, n * WIN, LANES), F32)

    def piece(n, dtype=BF):
        return ((keep, n * WIN, LANES), dtype)

    inner = (gain[0], qk[0], vt[0], wo[0], wgu[0], wd[0])
    early = call(
        bind(layer0_body, 0), [piece(parts[0], F32), piece(parts[0]), piece(parts[0])],
        far[0], xs[0], x, q, k, *inner, scratch=[buf(parts[0])],
    )
    fed_a, low_a, high_a = call(
        bind(layer0_body, parts[0]), [piece(first, F32), piece(first), piece(first)],
        far[1], xs[1], x, q, k, *inner, *early, scratch=[buf(parts[1])],
    )
    far_high_a = send(high_a, lambda t, f: (t, odd(f)))
    far_low_a = send(low_a, lambda t, f: ((t - 1) % tiles, odd(f)))
    fed_b, low_b, high_b, low = call(bind(layer0_last, first), [piece(rest, F32), piece(rest), piece(rest), piece(count)],
        far[2], xs[2], x, q, k, *inner, low_a, scratch=[buf(rest)],
    )
    below = send(low, lambda t, f: ((t - 1) % tiles, f))
    far_high_b = send(high_b, lambda t, f: (t, odd(f)))
    far_low_b = send(low_b, lambda t, f: ((t - 1) % tiles, odd(f)))
    whole = (count, size, LANES)
    x, xn, q, k = call(bind(own1_body), [(whole, F32), (whole, BF), (whole, BF), (whole, BF)],
        ends, fed_a, fed_b, below, wc[0], bias[0], gain[1], qk[1], scalars=1,
    )
    inner = (wc[0], bias[0], gain[0], gain[1], qk[1], vt[1], wo[1], wgu[1], wd[1])
    half = count // 2
    own_a, send_a = call(bind(layer1_first), [piece(half, F32), piece(half)],
        ends, far_high_a, far_low_a, xn, x, q, k, *inner, scratch=[buf(half)], scalars=1,
    )
    above_a = send(send_a, lambda t, f: ((t + 1) % tiles, f))
    own_b, send_b = call(bind(layer1_second), [piece(half, F32), piece(half)],
        ends, far_high_a, far_low_a, far_high_b, far_low_b, xn, x, q, k, *inner, scratch=[buf(half)], scalars=1,
    )
    above_b = send(send_b, lambda t, f: ((t + 1) % tiles, f))
    (out,) = call(bind(final_body), [((1, channels, rows, cols), BF)], ends, above_a, above_b, own_a, own_b, wc[1], bias[1], scalars=1)
    return out


def solution(mesh):
    in_specs = (P(("clips", "tm"), None, "tile", None), P(), P(), P(), P(), P(), P(), P(), P())
    out_specs = P(("clips", "tm"), None, "tile", None)
    return jax.shard_map(section, mesh=mesh, in_specs=in_specs, out_specs=out_specs, check_vma=False)
```

```python
import jax
import jax.numpy as jnp
from jax import lax
from jax.experimental import pallas as pl
from jax.experimental.pallas import tpu as pltpu
from jax.sharding import PartitionSpec as P


HEADS = 6
HD = 20
WIN = 8
LANES = 128
GROUP = 12
LEAD = 2
BF = jnp.bfloat16
F32 = jnp.float32
NT = (((1,), (1,)), ((), ()))


def up(n):
    return -(-n // LANES) * LANES


def dot(a, b):
    return jnp.dot(a, b, preferred_element_type=F32)


def dot_nt(a, b):
    return lax.dot_general(a, b, NT, preferred_element_type=F32)


def norm(x, gain, channels):
    lane = lax.broadcasted_iota(jnp.int32, x.shape, x.ndim - 1)
    mean = jnp.sum(x, axis=-1, keepdims=True) * (1.0 / channels)
    center = jnp.where(lane < channels, x - mean, 0.0)
    spread = jnp.sum(center * center, axis=-1, keepdims=True) * (1.0 / channels)
    return center * lax.rsqrt(spread + 1e-05) * gain


def to_positions(ref):
    x = ref[0].astype(F32)
    channels, rows, cols = x.shape
    x = jnp.concatenate([x, jnp.zeros((LANES - channels, rows, cols), F32)], axis=0)
    x = jnp.swapaxes(x, 0, 1)
    return jnp.stack([x[r].T for r in range(rows)], axis=0)


def windows(x):
    rows, cols, lanes = x.shape
    x = x.reshape(rows, cols // WIN, WIN, lanes)
    return jnp.swapaxes(x, 0, 1).reshape(cols // WIN, rows * WIN, lanes)


def unwindows(x, rows):
    count, _, lanes = x.shape
    x = jnp.swapaxes(x.reshape(count, rows, WIN, lanes), 0, 1)
    return x.reshape(rows, count * WIN, lanes)


def pad2(x, rows, cols):
    x = x.astype(F32)
    if x.shape[1] < cols:
        x = jnp.concatenate([x, jnp.zeros((x.shape[0], cols - x.shape[1]), F32)], axis=1)
    if x.shape[0] < rows:
        x = jnp.concatenate([x, jnp.zeros((rows - x.shape[0], cols), F32)], axis=0)
    return x


def norm_body(channels, x_hbm, *refs):
    x_ref, sems = refs[-2:]
    n = sems.shape[0] - 1
    params, o_x, o_parts, local = refs[:n], refs[n], refs[n + 1 : -2 - n], refs[-2 - n : -2]
    first = [pltpu.make_async_copy(x_hbm, x_ref, sems.at[n]), pltpu.make_async_copy(params[0], local[0], sems.at[0])]
    later = [pltpu.make_async_copy(params[i], local[i], sems.at[i]) for i in range(1, n)]
    for copy in first + later:
        copy.start()
    for copy in first:
        copy.wait()
    x = windows(to_positions(x_ref))
    o_x[...] = x
    xn = norm(x, pad2(local[0][0], 2, LANES)[:1], channels).astype(BF)
    at = 0
    for part in o_parts:
        part[...] = xn[at : at + part.shape[0]]
        at += part.shape[0]
    for copy in later:
        copy.wait()


def weights_body(channels, *refs):
    gain, qkv, out, gate, upw, down, conv, bias = refs[:8]
    layers = out.shape[0]
    xs, (o_q, o_k), outs = refs[8 : -2 - 8 * layers], refs[-2 - 8 * layers : -8 * layers], refs[-8 * layers :]
    hp = up(gate.shape[2])
    for l in range(layers):
        o_gain, o_qk, o_vt, o_out, o_gu, o_down, o_conv, o_bias = outs[8 * l : 8 * l + 8]
        o_gain[...] = pad2(gain[l], 2, LANES)
        o_bias[...] = pad2(bias[l : l + 1], 1, LANES)
        w = qkv[l].astype(F32)
        wq = pad2(w[:, :channels], LANES, LANES).astype(BF)
        wk = pad2(w[:, channels : 2 * channels], LANES, LANES).astype(BF)
        o_qk[:, :LANES] = wq
        o_qk[:, LANES:] = wk
        o_vt[...] = pad2(w[:, 2 * channels :], LANES, LANES).T.astype(BF)
        o_out[...] = pad2(out[l], LANES, LANES).astype(BF)
        o_gu[:, :hp] = pad2(gate[l], LANES, hp).astype(BF)
        o_gu[:, hp:] = pad2(upw[l], LANES, hp).astype(BF)
        o_down[...] = pad2(down[l], hp, LANES).astype(BF)
        blank = jnp.zeros((3 * LANES, LANES), BF)
        o_conv[3 * 3 * LANES :, :LANES] = blank
        o_conv[: 3 * LANES, LANES:] = blank
        for tap in range(9):
            a, b = divmod(tap, 3)
            piece = pad2(conv[l, tap], LANES, LANES).astype(BF)
            for v in range(2):
                at = ((a + v) * 3 + b) * LANES
                o_conv[at : at + LANES, v * LANES : (v + 1) * LANES] = piece
        if l == 0:
            project(jnp.concatenate([part[...] for part in xs], axis=0), jnp.concatenate([wq, wk], axis=1), o_q, o_k)


def project(xn, qk, o_q, o_k):
    count, size, _ = xn.shape
    both = dot(xn.reshape(count * size, LANES), qk).astype(BF)
    o_q[...] = both[:, :LANES].reshape(count, size, LANES)
    o_k[...] = both[:, LANES:].reshape(count, size, LANES)


def pieces(count):
    n = -(-count // GROUP)
    edges = [count * i // n for i in range(n + 1)]
    return [(a, b - a) for a, b in zip(edges, edges[1:])]


def pipeline(stages, total):
    held = [None] * (len(stages) + 1)
    for step in range(total + len(stages) - 1):
        for i in reversed(range(len(stages))):
            if 0 <= step - i < total:
                held[i + 1] = stages[i](step - i, held[i])


def mutual(channels, base, count, far, own, x_ref, q_ref, k_ref, gain, qk, vt, wo, wgu, wd, emit):
    size = x_ref.shape[1]
    hp = wd.shape[0]
    head_of = lax.broadcasted_iota(jnp.int32, (size, LANES), 1) // HD
    sub = lax.broadcasted_iota(jnp.int32, (LANES, LANES), 0) // HD
    half = lax.broadcasted_iota(jnp.int32, (LANES, LANES), 1) // size
    valid = (sub % 2 == half) & (sub < HEADS)
    scale = HD ** (-0.5) * 1.4426950408889634
    cuts = pieces(count)

    def fetch(g, _):
        at, n = cuts[g]
        fn = far(at, n)
        return fn, dot(fn.reshape(n * size, LANES), qk[:, LANES:]).astype(BF).reshape(n, size, LANES)

    def scores(g, state):
        fn, fk = state
        at, n = cuts[g]
        both = [jnp.concatenate([own[at + i], fn[i]], axis=0) for i in range(n)]
        vals = []
        for i in range(0, n, 2):
            pair = both[i : i + 2]
            v = dot_nt(vt[...], jnp.concatenate(pair, axis=0)).astype(BF)
            vals += [v[:, 2 * size * j : 2 * size * (j + 1)] for j in range(len(pair))]
        out = []
        for i in range(n):
            keys = jnp.concatenate([k_ref[base + at + i], fk[i]], axis=0)
            q = q_ref[base + at + i]
            qm = jnp.concatenate([jnp.where(head_of == h, q, jnp.zeros_like(q)) for h in range(HEADS)], axis=0)
            out.append((vals[i], dot_nt(keys, qm)))
        return out

    def attend(g, state):
        out = []
        for vals, s in state:
            top = jnp.max(s, axis=0, keepdims=True)
            p = jnp.exp2((s - top) * scale)
            p = (p * (1.0 / jnp.sum(p, axis=0, keepdims=True))).astype(BF)
            cut = 4 * HD
            out.append((dot(vals[:cut], p[:, : 4 * size]), dot(vals[cut:], p[:, 4 * size :])))
        return out

    def merge(g, state):
        mixed = []
        for front, back in state:
            two = 2 * HD
            r = jnp.concatenate([front[:two, :LANES], front[two:, LANES:], back], axis=0)
            r = jnp.where(valid, r, 0.0).T
            mixed.append(r[:size] + r[size:])
        mixed = jnp.concatenate(mixed, axis=0).astype(BF)
        at, n = cuts[g]
        return x_ref[base + at : base + at + n].reshape(n * size, LANES) + dot(mixed, wo[...])

    def widen(g, att):
        nf = norm(att, gain[1:2], channels).astype(BF)
        return att, dot(nf, wgu[...])

    def narrow(g, state):
        att, gu = state
        gate = gu[:, :hp]
        act = 0.5 * gate * (1.0 + lax.erf(gate * (0.5**0.5))) * gu[:, hp:]
        fed = att + dot(act.astype(BF), wd[...])
        at, n = cuts[g]
        emit(at, fed.reshape(n, size, LANES))

    pipeline([fetch, scores, attend, merge, widen, narrow], len(cuts))


def conv_rows(x, shift, origin, edge, wc, bias):
    cols = x.shape[1]
    taps = [pltpu.roll(x, (shift + 1 - b) % cols, 1) if (shift + 1 - b) % cols else x for b in range(3)]
    return conv_taps(taps, origin, cols, edge, wc, bias)


def conv_cols(x, skip, origin, cols, edge, wc, bias):
    n = x.shape[1] - 2 * skip
    taps = [x[:, skip - 1 + b : skip - 1 + b + n] for b in range(3)]
    return conv_taps(taps, origin, cols, edge, wc, bias)


def conv_taps(taps, origin, cols, edge, wc, bias):
    center = taps[1]
    rows, width = center.shape[0] - 2, center.shape[1]
    col = (lax.broadcasted_iota(jnp.int32, (width, 1), 0) + origin) % cols
    parts = []
    for b, moved in enumerate(taps):
        if b != 1:
            moved = jnp.where(col == (0 if b == 0 else cols - 1), 0.0, moved)
        parts.append(moved)
    lines = [jnp.concatenate([p[r] for p in parts], axis=1) for r in range(rows + 2)]
    packed = [line.astype(BF) for line in lines]
    blocks = []
    for j in range(rows // 2):
        four = packed[2 * j : 2 * j + 4]
        if edge is not None:
            last, at = edge
            if 2 * j + 1 == at - 1:
                four[3] = jnp.where(last, 0.0, lines[2 * j + 3]).astype(BF)
            if 2 * j == at:
                four[0] = jnp.where(last, 0.0, lines[2 * j]).astype(BF)
        blocks.append(jnp.concatenate(four, axis=1))
    if width == cols:
        lhs = jnp.concatenate(blocks, axis=0)
        mid = lhs.shape[1] // 2
        both = dot(lhs[:, :mid], wc[:mid, :]) + dot(lhs[:, mid:], wc[mid:, :])
    else:
        mid = len(blocks) // 2
        both = [dot(jnp.concatenate(b, axis=0), wc[...]) for b in (blocks[:mid], blocks[mid:])]
        both = jnp.concatenate(both, axis=0)
    out = []
    for r in range(rows):
        j, v = divmod(r, 2)
        part = both[j * width : (j + 1) * width, v * LANES : (v + 1) * LANES]
        out.append(center[1 + r] + bias[...] + part)
    return jnp.stack(out, axis=0)


def packing(groups, channels):
    spare = LANES - channels
    if spare == 0 or channels % spare:
        return 0, 1
    per = channels // spare
    return groups // (per + 1), per


def packed_rows(shape, channels):
    groups = shape[0] * shape[1] // WIN
    return ((groups - packing(groups, channels)[0]) * WIN, LANES)


def pack(x, channels):
    groups = x.shape[0] * x.shape[1] // WIN
    extra, per = packing(groups, channels)
    x = x.reshape(groups, WIN, LANES)
    lane = lax.broadcasted_iota(jnp.int32, (WIN, LANES), 1)
    out = []
    for c in range(groups - extra):
        e, i = divmod(c, per)
        line = x[c]
        if e < extra:
            turn = (channels - (LANES - channels) * i) % LANES
            moved = pltpu.roll(x[groups - extra + e], turn, 1) if turn else x[groups - extra + e]
            line = jnp.where(lane < channels, line, moved)
        out.append(line)
    return jnp.concatenate(out, axis=0).astype(BF)


def unpack(y, rows, channels):
    y = y.astype(F32).reshape(-1, WIN, LANES)
    groups = next(g for g in range(y.shape[0], 2 * y.shape[0] + 1) if g - packing(g, channels)[0] == y.shape[0] and g % rows == 0)
    extra, per = packing(groups, channels)
    spare = LANES - channels
    lane = lax.broadcasted_iota(jnp.int32, (WIN, LANES), 1)
    out, tails = [], []
    for c in range(groups - extra):
        e, i = divmod(c, per)
        if e >= extra:
            out.append(y[c])
            continue
        out.append(jnp.where(lane < channels, y[c], 0.0))
        turn = (spare * i - channels) % LANES
        moved = pltpu.roll(y[c], turn, 1) if turn else y[c]
        if i == 0:
            tails.append(jnp.where(lane < spare, moved, 0.0))
        else:
            tails[e] = jnp.where((lane >= spare * i) & (lane < spare * (i + 1)), moved, tails[e])
    return jnp.stack(out + tails, axis=0).reshape(rows, groups // rows * WIN, LANES)


def collect(buf):
    def emit(at, fed):
        buf[:, at * WIN : (at + fed.shape[0]) * WIN, :] = unwindows(fed, buf.shape[0])

    return emit


def layer0_first(channels, far, own, x_ref, q_ref, k_ref, gain, qk, vt, wo, wgu, wd, o_fed, o_low, buf):
    rows, keep = buf.shape[0], o_low.shape[0]
    mutual(channels, 0, far.shape[0], lambda at, n: far[at : at + n], own, x_ref, q_ref, k_ref, gain, qk, vt, wo, wgu, wd, collect(buf))
    o_fed[...] = buf[rows - keep :]
    o_low[...] = buf[:keep].astype(BF)


def layer0_middle(channels, base, far, own, x_ref, q_ref, k_ref, gain, qk, vt, wo, wgu, wd, fed_a, low_a, o_fed, o_low, o_plow, o_phigh, buf):
    rows, keep = buf.shape[0], o_low.shape[0]
    mutual(channels, base, far.shape[0], lambda at, n: far[at : at + n], own, x_ref, q_ref, k_ref, gain, qk, vt, wo, wgu, wd, collect(buf))
    fed = jnp.concatenate([fed_a[...], buf[rows - keep :]], axis=1)
    low = jnp.concatenate([low_a[...].astype(F32), buf[:keep]], axis=1)
    o_fed[...] = fed
    o_low[...] = low.astype(BF)
    o_plow[...] = pack(low, channels)
    o_phigh[...] = pack(fed, channels)


def layer0_last(channels, base, far, own, x_ref, q_ref, k_ref, gain, qk, vt, wo, wgu, wd, low_a, o_fed, o_plow, o_phigh, o_low, buf):
    rows, keep = buf.shape[0], o_low.shape[0]
    mutual(channels, base, far.shape[0], lambda at, n: far[at : at + n], own, x_ref, q_ref, k_ref, gain, qk, vt, wo, wgu, wd, collect(buf))
    fed, low = buf[rows - keep :], buf[:keep]
    o_fed[...] = fed
    o_plow[...] = pack(low, channels)
    o_phigh[...] = pack(fed, channels)
    first = base * WIN
    o_low[:, :first, :] = low_a[...]
    o_low[:, first:, :] = low.astype(BF)


def own1_body(channels, ends, fed_a, fed_b, low, wc, bias, gain, qk, o_x, o_xn, o_q, o_k):
    high = jnp.concatenate([fed_a[...], fed_b[...]], axis=1)
    x = jnp.concatenate([high, low[...].astype(F32)], axis=0)
    cols = x.shape[1]
    x = jnp.concatenate([x, x[:, :WIN]], axis=1)
    cuts = [(0, cols // WIN)]

    def mix(g, _):
        at, n = cuts[g]
        part = x[:, at * WIN : (at + n + 1) * WIN]
        return windows(conv_cols(part, WIN // 2, at * WIN + WIN // 2, cols, (ends[0] == 1, WIN // 2), wc, bias))

    def finish(g, part):
        at, n = cuts[g]
        o_x[at : at + n] = part
        xn = norm(part, gain[0:1], channels).astype(BF)
        o_xn[at : at + n] = xn
        project(xn, qk[...], o_q.at[at : at + n], o_k.at[at : at + n])

    pipeline([mix, finish], len(cuts))


def far_normed(channels, ends, x, base, cols, wc, bias, gain):
    def far(at, n):
        part = x[:, at * WIN : (at + n + 1) * WIN]
        part = conv_cols(part, WIN // 2, base + at * WIN + WIN // 2, cols, (ends[0] == 1, WIN // 2), wc, bias)
        return norm(windows(part), gain[0:1], channels).astype(BF)

    return far


def layer1_first(channels, ends, high, low, xn_ref, x_ref, q_ref, k_ref, wc, bias, gain0, gain, qk, vt, wo, wgu, wd, o_own, o_send, buf):
    rows, keep = buf.shape[0], o_own.shape[0]
    x = jnp.concatenate([unpack(high[...], keep, channels), unpack(low[...], keep, channels)], axis=0)
    count = buf.shape[1] // WIN
    far = far_normed(channels, ends, x, 0, x_ref.shape[0] * WIN, wc, bias, gain)
    mutual(channels, 0, count, far, xn_ref, x_ref, q_ref, k_ref, gain, qk, vt, wo, wgu, wd, collect(buf))
    o_own[...] = buf[:keep]
    o_send[...] = buf[rows - keep :].astype(BF)


def layer1_second(channels, ends, high_a, low_a, high_b, low_b, xn_ref, x_ref, q_ref, k_ref, wc, bias, gain0, gain, qk, vt, wo, wgu, wd, o_own, o_send, buf):
    keep = o_own.shape[0]
    xa = jnp.concatenate([unpack(part[...], keep, channels) for part in (high_a, low_a)], axis=0)
    xb = jnp.concatenate([unpack(part[...], keep, channels) for part in (high_b, low_b)], axis=0)
    cols = x_ref.shape[0] * WIN
    base = cols - buf.shape[1]
    x = jnp.concatenate([xa[:, base:], xb, xa[:, :WIN]], axis=1)
    rows, at, count = buf.shape[0], base // WIN, buf.shape[1] // WIN
    far = far_normed(channels, ends, x, base, cols, wc, bias, gain)
    mutual(channels, at, count, far, xn_ref.at[at:], x_ref, q_ref, k_ref, gain, qk, vt, wo, wgu, wd, collect(buf))
    o_own[...] = buf[:keep]
    o_send[...] = buf[rows - keep :].astype(BF)


def final_body(channels, ends, high_a, high_b, own_a, own_b, wc, bias, o_hbm, out, sems):
    first, last = ends[1] == 1, ends[0] == 1
    high = jnp.concatenate([high_a[...], high_b[...]], axis=1).astype(F32)
    own = jnp.concatenate([own_a[...], own_b[...]], axis=1)
    top = jnp.where(first, 0.0, high[:1])
    low = jnp.where(last, 0.0, own[-1:])
    x = jnp.concatenate([top, high[1:], own[:-1], low], axis=0)
    y = conv_rows(x, WIN // 2, 0, None, wc, bias)
    y = jnp.stack([y[r].T for r in range(y.shape[0])], axis=0)
    copies = []
    n = sems.shape[0]
    step = channels // n
    for i in range(n):
        at = i * step
        out[0, at : at + step] = jnp.swapaxes(y[:, at : at + step], 0, 1).astype(BF)
        copy = pltpu.make_async_copy(out.at[0, at : at + step], o_hbm.at[0, at : at + step], sems.at[i])
        copy.start()
        copies.append(copy)
    for copy in copies:
        copy.wait()


def call(body, outs, *args, scratch=(), scalars=0, remote=0, away=False):
    vm = pl.BlockSpec(memory_space=pltpu.VMEM)
    sm = pl.BlockSpec(memory_space=pltpu.SMEM)
    hbm = pl.BlockSpec(memory_space=pltpu.HBM)
    specs = [sm] * scalars + [hbm] * remote
    run = pl.pallas_call(
        body,
        out_shape=[jax.ShapeDtypeStruct(s, d) for s, d in outs],
        in_specs=specs + [vm] * (len(args) - len(specs)),
        out_specs=[hbm if away else vm] * len(outs),
        scratch_shapes=list(scratch),
        compiler_params=pltpu.CompilerParams(vmem_limit_bytes=24 * 1024 * 1024),
    )
    args = [pltpu.with_memory_space_constraint(a, pltpu.HBM) if i < scalars + remote and i >= scalars else a for i, a in enumerate(args)]
    return run(*args)


def section(frames, *params):
    ln_gain, gate_weight = params[0], params[3]
    _, channels, rows, cols = frames.shape
    layers = ln_gain.shape[0]
    hp = up(gate_weight.shape[2])
    tiles, depth = lax.axis_size("tile"), lax.axis_size("tm")
    where = lax.axis_index("tile")
    ends = jnp.stack([where == tiles - 1, where == 0]).astype(jnp.int32)
    axes = ("tile", "tm")

    def odd(f):
        return (f + 1) % depth if f % 2 else (f - 1) % depth

    def send(x, target):
        pairs = []
        for t in range(tiles):
            for f in range(depth):
                to_t, to_f = target(t, f)
                pairs.append((t * depth + f, to_t * depth + to_f))
        return lax.ppermute(x, axes, pairs)

    def bind(body, *extra):
        def wrapped(*refs):
            return body(channels, *extra, *refs)

        wrapped.__name__ = body.__name__
        return wrapped

    count = cols // WIN
    first = count // 2 + LEAD
    rest = count - first
    keep = rows // 2 + 1
    size = rows * WIN
    dma = pltpu.SemaphoreType.DMA
    parts = [-(-first // 2), first // 2, rest]
    x, *xs = call(
        bind(norm_body),
        [((count, size, LANES), F32)] + [((n, size, LANES), BF) for n in parts] + [(p.shape, p.dtype) for p in params],
        frames, *params,
        scratch=[pltpu.VMEM(frames.shape, BF), dma((1 + len(params),))],
        remote=1 + len(params),
    )
    xs, params = xs[: len(parts)], xs[len(parts) :]
    far = [send(part, lambda t, f: (t, f ^ 1)) for part in xs]
    q, k, *sets = call(bind(weights_body),
        [((count, size, LANES), BF), ((count, size, LANES), BF)]
        + [
            ((2, LANES), F32),
            ((LANES, 2 * LANES), BF),
            ((LANES, LANES), BF),
            ((LANES, LANES), BF),
            ((LANES, 2 * hp), BF),
            ((hp, LANES), BF),
            ((12 * LANES, 2 * LANES), BF),
            ((1, LANES), F32),
        ]
        * layers,
        *params, *xs,
    )

    gain, qk, vt, wo, wgu, wd, wc, bias = zip(*[sets[8 * l : 8 * l + 8] for l in range(layers)])

    def buf(n):
        return pltpu.VMEM((rows, n * WIN, LANES), F32)

    def piece(n, dtype=BF):
        return ((keep, n * WIN, LANES), dtype)

    inner = (gain[0], qk[0], vt[0], wo[0], wgu[0], wd[0])

    def thin(n):
        return (packed_rows(piece(n)[0], channels), BF)

    early = call(
        bind(layer0_first), [piece(parts[0], F32), piece(parts[0])],
        far[0], xs[0], x, q, k, *inner, scratch=[buf(parts[0])],
    )
    fed_a, low, low_a, high_a = call(
        bind(layer0_middle, parts[0]), [piece(first, F32), piece(first), thin(first), thin(first)],
        far[1], xs[1], x, q, k, *inner, *early, scratch=[buf(parts[1])],
    )
    far_high_a = send(high_a, lambda t, f: (t, odd(f)))
    far_low_a = send(low_a, lambda t, f: ((t - 1) % tiles, odd(f)))
    fed_b, low_b, high_b, low = call(bind(layer0_last, first), [piece(rest, F32), thin(rest), thin(rest), piece(count)],
        far[2], xs[2], x, q, k, *inner, low, scratch=[buf(rest)],
    )
    below = send(low, lambda t, f: ((t - 1) % tiles, f))
    far_high_b = send(high_b, lambda t, f: (t, odd(f)))
    far_low_b = send(low_b, lambda t, f: ((t - 1) % tiles, odd(f)))
    whole = (count, size, LANES)
    x, xn, q, k = call(bind(own1_body), [(whole, F32), (whole, BF), (whole, BF), (whole, BF)],
        ends, fed_a, fed_b, below, wc[0], bias[0], gain[1], qk[1], scalars=1,
    )
    inner = (wc[0], bias[0], gain[0], gain[1], qk[1], vt[1], wo[1], wgu[1], wd[1])
    half = first - 1
    own_a, send_a = call(bind(layer1_first), [piece(half, F32), piece(half)],
        ends, far_high_a, far_low_a, xn, x, q, k, *inner, scratch=[buf(half)], scalars=1,
    )
    above_a = send(send_a, lambda t, f: ((t + 1) % tiles, f))
    own_b, send_b = call(bind(layer1_second), [piece(count - half, F32), piece(count - half)],
        ends, far_high_a, far_low_a, far_high_b, far_low_b, xn, x, q, k, *inner, scratch=[buf(count - half)], scalars=1,
    )
    above_b = send(send_b, lambda t, f: ((t + 1) % tiles, f))
    (out,) = call(bind(final_body), [((1, channels, rows, cols), BF)], ends, above_a, above_b, own_a, own_b, wc[1], bias[1],
        scratch=[pltpu.VMEM(frames.shape, BF), dma((5,))], scalars=1, away=True,
    )
    return out


def solution(mesh):
    in_specs = (P(("clips", "tm"), None, "tile", None), P(), P(), P(), P(), P(), P(), P(), P())
    out_specs = P(("clips", "tm"), None, "tile", None)
    return jax.shard_map(section, mesh=mesh, in_specs=in_specs, out_specs=out_specs, check_vma=False)
```

```python
import jax
import jax.numpy as jnp
from jax import lax
from jax.experimental import pallas as pl
from jax.experimental.pallas import tpu as pltpu
from jax.sharding import PartitionSpec as P


HEADS = 6
HD = 20
WIN = 8
LANES = 128
GROUP = 12
LEAD = 2
BF = jnp.bfloat16
F32 = jnp.float32
NT = (((1,), (1,)), ((), ()))


def up(n):
    return -(-n // LANES) * LANES


def dot(a, b):
    return jnp.dot(a, b, preferred_element_type=F32)


def dot_nt(a, b):
    return lax.dot_general(a, b, NT, preferred_element_type=F32)


def norm(x, gain, channels):
    lane = lax.broadcasted_iota(jnp.int32, x.shape, x.ndim - 1)
    mean = jnp.sum(x, axis=-1, keepdims=True) * (1.0 / channels)
    center = jnp.where(lane < channels, x - mean, 0.0)
    spread = jnp.sum(center * center, axis=-1, keepdims=True) * (1.0 / channels)
    return center * lax.rsqrt(spread + 1e-05) * gain


def to_positions(ref):
    x = ref[0].astype(F32)
    channels, rows, cols = x.shape
    x = jnp.concatenate([x, jnp.zeros((LANES - channels, rows, cols), F32)], axis=0)
    x = jnp.swapaxes(x, 0, 1)
    return jnp.stack([x[r].T for r in range(rows)], axis=0)


def windows(x):
    rows, cols, lanes = x.shape
    x = x.reshape(rows, cols // WIN, WIN, lanes)
    return jnp.swapaxes(x, 0, 1).reshape(cols // WIN, rows * WIN, lanes)


def unwindows(x, rows):
    count, _, lanes = x.shape
    x = jnp.swapaxes(x.reshape(count, rows, WIN, lanes), 0, 1)
    return x.reshape(rows, count * WIN, lanes)


def pad2(x, rows, cols):
    x = x.astype(F32)
    if x.shape[1] < cols:
        x = jnp.concatenate([x, jnp.zeros((x.shape[0], cols - x.shape[1]), F32)], axis=1)
    if x.shape[0] < rows:
        x = jnp.concatenate([x, jnp.zeros((rows - x.shape[0], cols), F32)], axis=0)
    return x


def norm_body(channels, x_hbm, *refs):
    x_ref, sems = refs[-2:]
    n = sems.shape[0] - 1
    params, o_x, o_parts, local = refs[:n], refs[n], refs[n + 1 : -2 - n], refs[-2 - n : -2]
    first = [pltpu.make_async_copy(x_hbm, x_ref, sems.at[n]), pltpu.make_async_copy(params[0], local[0], sems.at[0])]
    later = [pltpu.make_async_copy(params[i], local[i], sems.at[i]) for i in range(1, n)]
    for copy in first + later:
        copy.start()
    for copy in first:
        copy.wait()
    x = windows(to_positions(x_ref))
    o_x[...] = x
    xn = norm(x, pad2(local[0][0], 2, LANES)[:1], channels).astype(BF)
    at = 0
    for part in o_parts:
        part[...] = xn[at : at + part.shape[0]]
        at += part.shape[0]
    for copy in later:
        copy.wait()


def weights_body(channels, *refs):
    gain, qkv, out, gate, upw, down, conv, bias = refs[:8]
    layers = out.shape[0]
    xs, (o_q, o_k), outs = refs[8 : -2 - 8 * layers], refs[-2 - 8 * layers : -8 * layers], refs[-8 * layers :]
    hp = up(gate.shape[2])
    for l in range(layers):
        o_gain, o_qk, o_vt, o_out, o_gu, o_down, o_conv, o_bias = outs[8 * l : 8 * l + 8]
        o_gain[...] = pad2(gain[l], 2, LANES)
        o_bias[...] = pad2(bias[l : l + 1], 1, LANES)
        w = qkv[l].astype(F32)
        wq = pad2(w[:, :channels], LANES, LANES).astype(BF)
        wk = pad2(w[:, channels : 2 * channels], LANES, LANES).astype(BF)
        o_qk[:, :LANES] = wq
        o_qk[:, LANES:] = wk
        o_vt[...] = pad2(w[:, 2 * channels :], LANES, LANES).T.astype(BF)
        o_out[...] = pad2(out[l], LANES, LANES).astype(BF)
        o_gu[:, :hp] = pad2(gate[l], LANES, hp).astype(BF)
        o_gu[:, hp:] = pad2(upw[l], LANES, hp).astype(BF)
        o_down[...] = pad2(down[l], hp, LANES).astype(BF)
        blank = jnp.zeros((3 * LANES, LANES), BF)
        o_conv[3 * 3 * LANES :, :LANES] = blank
        o_conv[: 3 * LANES, LANES:] = blank
        for tap in range(9):
            a, b = divmod(tap, 3)
            piece = pad2(conv[l, tap], LANES, LANES).astype(BF)
            for v in range(2):
                at = ((a + v) * 3 + b) * LANES
                o_conv[at : at + LANES, v * LANES : (v + 1) * LANES] = piece
        if l == 0:
            project(jnp.concatenate([part[...] for part in xs], axis=0), jnp.concatenate([wq, wk], axis=1), o_q, o_k)


def project(xn, qk, o_q, o_k):
    count, size, _ = xn.shape
    both = dot(xn.reshape(count * size, LANES), qk).astype(BF)
    o_q[...] = both[:, :LANES].reshape(count, size, LANES)
    o_k[...] = both[:, LANES:].reshape(count, size, LANES)


def pieces(count):
    n = -(-count // GROUP)
    edges = [count * i // n for i in range(n + 1)]
    return [(a, b - a) for a, b in zip(edges, edges[1:])]


def pipeline(stages, total):
    held = [None] * (len(stages) + 1)
    for step in range(total + len(stages) - 1):
        for i in reversed(range(len(stages))):
            if 0 <= step - i < total:
                held[i + 1] = stages[i](step - i, held[i])


def mutual(channels, base, count, far, own, x_ref, q_ref, k_ref, gain, qk, vt, wo, wgu, wd, emit):
    size = x_ref.shape[1]
    hp = wd.shape[0]
    head_of = lax.broadcasted_iota(jnp.int32, (size, LANES), 1) // HD
    sub = lax.broadcasted_iota(jnp.int32, (LANES, LANES), 0) // HD
    half = lax.broadcasted_iota(jnp.int32, (LANES, LANES), 1) // size
    valid = (sub % 2 == half) & (sub < HEADS)
    scale = HD ** (-0.5) * 1.4426950408889634
    cuts = pieces(count)

    def fetch(g, _):
        at, n = cuts[g]
        fn = far(at, n)
        return fn, dot(fn.reshape(n * size, LANES), qk[:, LANES:]).astype(BF).reshape(n, size, LANES)

    def scores(g, state):
        fn, fk = state
        at, n = cuts[g]
        both = [jnp.concatenate([own[at + i], fn[i]], axis=0) for i in range(n)]
        vals = []
        for i in range(0, n, 2):
            pair = both[i : i + 2]
            v = dot_nt(vt[...], jnp.concatenate(pair, axis=0)).astype(BF)
            vals += [v[:, 2 * size * j : 2 * size * (j + 1)] for j in range(len(pair))]
        out = []
        for i in range(n):
            keys = jnp.concatenate([k_ref[base + at + i], fk[i]], axis=0)
            q = q_ref[base + at + i]
            qm = jnp.concatenate([jnp.where(head_of == h, q, jnp.zeros_like(q)) for h in range(HEADS)], axis=0)
            out.append((vals[i], dot_nt(keys, qm)))
        return out

    def attend(g, state):
        out = []
        for vals, s in state:
            top = jnp.max(s, axis=0, keepdims=True)
            p = jnp.exp2((s - top) * scale)
            p = (p * (1.0 / jnp.sum(p, axis=0, keepdims=True))).astype(BF)
            cut = 4 * HD
            out.append((dot(vals[:cut], p[:, : 4 * size]), dot(vals[cut:], p[:, 4 * size :])))
        return out

    def merge(g, state):
        mixed = []
        for front, back in state:
            two = 2 * HD
            r = jnp.concatenate([front[:two, :LANES], front[two:, LANES:], back], axis=0)
            r = jnp.where(valid, r, 0.0).T
            mixed.append(r[:size] + r[size:])
        mixed = jnp.concatenate(mixed, axis=0).astype(BF)
        at, n = cuts[g]
        return x_ref[base + at : base + at + n].reshape(n * size, LANES) + dot(mixed, wo[...])

    def widen(g, att):
        nf = norm(att, gain[1:2], channels).astype(BF)
        return att, dot(nf, wgu[...])

    def narrow(g, state):
        att, gu = state
        gate = gu[:, :hp]
        act = 0.5 * gate * (1.0 + lax.erf(gate * (0.5**0.5))) * gu[:, hp:]
        fed = att + dot(act.astype(BF), wd[...])
        at, n = cuts[g]
        emit(at, fed.reshape(n, size, LANES))

    pipeline([fetch, scores, attend, merge, widen, narrow], len(cuts))


def conv_cols(x, skip, origin, cols, edge, wc, bias):
    n = x.shape[1] - 2 * skip
    taps = [x[:, skip - 1 + b : skip - 1 + b + n] for b in range(3)]
    return conv_taps(taps, origin, cols, edge, wc, bias)


def conv_taps(taps, origin, cols, edge, wc, bias):
    center = taps[1]
    rows, width = center.shape[0] - 2, center.shape[1]
    col = (lax.broadcasted_iota(jnp.int32, (width, 1), 0) + origin) % cols
    parts = []
    for b, moved in enumerate(taps):
        if b != 1:
            moved = jnp.where(col == (0 if b == 0 else cols - 1), 0.0, moved)
        parts.append(moved)
    lines = [jnp.concatenate([p[r] for p in parts], axis=1) for r in range(rows + 2)]
    packed = [line.astype(BF) for line in lines]
    blocks = []
    for j in range(rows // 2):
        four = packed[2 * j : 2 * j + 4]
        if edge is not None:
            last, at = edge
            if 2 * j + 1 == at - 1:
                four[3] = jnp.where(last, 0.0, lines[2 * j + 3]).astype(BF)
            if 2 * j == at:
                four[0] = jnp.where(last, 0.0, lines[2 * j]).astype(BF)
        blocks.append(jnp.concatenate(four, axis=1))
    if width == cols:
        lhs = jnp.concatenate(blocks, axis=0)
        mid = lhs.shape[1] // 2
        both = dot(lhs[:, :mid], wc[:mid, :]) + dot(lhs[:, mid:], wc[mid:, :])
    else:
        mid = len(blocks) // 2
        both = [dot(jnp.concatenate(b, axis=0), wc[...]) for b in (blocks[:mid], blocks[mid:])]
        both = jnp.concatenate(both, axis=0)
    out = []
    for r in range(rows):
        j, v = divmod(r, 2)
        part = both[j * width : (j + 1) * width, v * LANES : (v + 1) * LANES]
        out.append(center[1 + r] + bias[...] + part)
    return jnp.stack(out, axis=0)


def packing(groups, channels):
    spare = LANES - channels
    if spare == 0 or channels % spare:
        return 0, 1
    per = channels // spare
    return groups // (per + 1), per


def packed_rows(shape, channels):
    groups = shape[0] * shape[1] // WIN
    return ((groups - packing(groups, channels)[0]) * WIN, LANES)


def pack(x, channels):
    groups = x.shape[0] * x.shape[1] // WIN
    extra, per = packing(groups, channels)
    x = x.reshape(groups, WIN, LANES)
    lane = lax.broadcasted_iota(jnp.int32, (WIN, LANES), 1)
    out = []
    for c in range(groups - extra):
        e, i = divmod(c, per)
        line = x[c]
        if e < extra:
            turn = (channels - (LANES - channels) * i) % LANES
            moved = pltpu.roll(x[groups - extra + e], turn, 1) if turn else x[groups - extra + e]
            line = jnp.where(lane < channels, line, moved)
        out.append(line)
    return jnp.concatenate(out, axis=0).astype(BF)


def unpack(y, rows, channels):
    y = y.astype(F32).reshape(-1, WIN, LANES)
    groups = next(g for g in range(y.shape[0], 2 * y.shape[0] + 1) if g - packing(g, channels)[0] == y.shape[0] and g % rows == 0)
    extra, per = packing(groups, channels)
    spare = LANES - channels
    lane = lax.broadcasted_iota(jnp.int32, (WIN, LANES), 1)
    out, tails = [], []
    for c in range(groups - extra):
        e, i = divmod(c, per)
        if e >= extra:
            out.append(y[c])
            continue
        out.append(jnp.where(lane < channels, y[c], 0.0))
        turn = (spare * i - channels) % LANES
        moved = pltpu.roll(y[c], turn, 1) if turn else y[c]
        if i == 0:
            tails.append(jnp.where(lane < spare, moved, 0.0))
        else:
            tails[e] = jnp.where((lane >= spare * i) & (lane < spare * (i + 1)), moved, tails[e])
    return jnp.stack(out + tails, axis=0).reshape(rows, groups // rows * WIN, LANES)


def collect(buf):
    def emit(at, fed):
        buf[:, at * WIN : (at + fed.shape[0]) * WIN, :] = unwindows(fed, buf.shape[0])

    return emit


def layer0_first(channels, far, own, x_ref, q_ref, k_ref, gain, qk, vt, wo, wgu, wd, o_fed, o_low, buf):
    rows, keep = buf.shape[0], o_low.shape[0]
    mutual(channels, 0, far.shape[0], lambda at, n: far[at : at + n], own, x_ref, q_ref, k_ref, gain, qk, vt, wo, wgu, wd, collect(buf))
    o_fed[...] = buf[rows - keep :]
    o_low[...] = buf[:keep].astype(BF)


def layer0_middle(channels, base, far, own, x_ref, q_ref, k_ref, gain, qk, vt, wo, wgu, wd, fed_a, low_a, o_fed, o_low, o_plow, o_phigh, buf):
    rows, keep = buf.shape[0], o_low.shape[0]
    mutual(channels, base, far.shape[0], lambda at, n: far[at : at + n], own, x_ref, q_ref, k_ref, gain, qk, vt, wo, wgu, wd, collect(buf))
    fed = jnp.concatenate([fed_a[...], buf[rows - keep :]], axis=1)
    low = jnp.concatenate([low_a[...].astype(F32), buf[:keep]], axis=1)
    o_fed[...] = fed
    o_low[...] = low.astype(BF)
    o_plow[...] = pack(low, channels)
    o_phigh[...] = pack(fed, channels)


def layer0_last(channels, base, far, own, x_ref, q_ref, k_ref, gain, qk, vt, wo, wgu, wd, low_a, o_fed, o_plow, o_phigh, o_low, buf):
    rows, keep = buf.shape[0], o_low.shape[0]
    mutual(channels, base, far.shape[0], lambda at, n: far[at : at + n], own, x_ref, q_ref, k_ref, gain, qk, vt, wo, wgu, wd, collect(buf))
    fed, low = buf[rows - keep :], buf[:keep]
    o_fed[...] = fed
    o_plow[...] = pack(low, channels)
    o_phigh[...] = pack(fed, channels)
    first = base * WIN
    o_low[:, :first, :] = low_a[...]
    o_low[:, first:, :] = low.astype(BF)


def own1_body(channels, ends, fed_a, fed_b, low, wc, bias, gain, qk, o_x, o_xn, o_q, o_k):
    high = jnp.concatenate([fed_a[...], fed_b[...]], axis=1)
    x = jnp.concatenate([high, low[...].astype(F32)], axis=0)
    cols = x.shape[1]
    x = jnp.concatenate([x, x[:, :WIN]], axis=1)
    cuts = [(0, cols // WIN)]

    def mix(g, _):
        at, n = cuts[g]
        part = x[:, at * WIN : (at + n + 1) * WIN]
        return windows(conv_cols(part, WIN // 2, at * WIN + WIN // 2, cols, (ends[0] == 1, WIN // 2), wc, bias))

    def finish(g, part):
        at, n = cuts[g]
        o_x[at : at + n] = part
        xn = norm(part, gain[0:1], channels).astype(BF)
        o_xn[at : at + n] = xn
        project(xn, qk[...], o_q.at[at : at + n], o_k.at[at : at + n])

    pipeline([mix, finish], len(cuts))


def far_normed(channels, ends, x, base, cols, wc, bias, gain):
    def far(at, n):
        part = x[:, at * WIN : (at + n + 1) * WIN]
        part = conv_cols(part, WIN // 2, base + at * WIN + WIN // 2, cols, (ends[0] == 1, WIN // 2), wc, bias)
        return norm(windows(part), gain[0:1], channels).astype(BF)

    return far


def layer1_first(channels, ends, high, low, xn_ref, x_ref, q_ref, k_ref, wc, bias, gain0, gain, qk, vt, wo, wgu, wd, o_own, o_send, buf):
    rows, keep = buf.shape[0], o_own.shape[0]
    x = jnp.concatenate([unpack(high[...], keep, channels), unpack(low[...], keep, channels)], axis=0)
    count = buf.shape[1] // WIN
    far = far_normed(channels, ends, x, 0, x_ref.shape[0] * WIN, wc, bias, gain)
    mutual(channels, 0, count, far, xn_ref, x_ref, q_ref, k_ref, gain, qk, vt, wo, wgu, wd, collect(buf))
    o_own[...] = buf[:keep]
    o_send[...] = buf[rows - keep :].astype(BF)


def layer1_second(channels, ends, high_a, low_a, high_b, low_b, xn_ref, x_ref, q_ref, k_ref, wc, bias, gain0, gain, qk, vt, wo, wgu, wd, o_own, o_send, buf):
    keep = o_own.shape[0]
    xa = jnp.concatenate([unpack(part[...], keep, channels) for part in (high_a, low_a)], axis=0)
    xb = jnp.concatenate([unpack(part[...], keep, channels) for part in (high_b, low_b)], axis=0)
    cols = x_ref.shape[0] * WIN
    base = cols - buf.shape[1]
    x = jnp.concatenate([xa[:, base:], xb, xa[:, :WIN]], axis=1)
    rows, at, count = buf.shape[0], base // WIN, buf.shape[1] // WIN
    far = far_normed(channels, ends, x, base, cols, wc, bias, gain)
    mutual(channels, at, count, far, xn_ref.at[at:], x_ref, q_ref, k_ref, gain, qk, vt, wo, wgu, wd, collect(buf))
    o_own[...] = buf[:keep]
    o_send[...] = buf[rows - keep :].astype(BF)


def lines_of(x, shift):
    cols = x.shape[1]
    col = lax.broadcasted_iota(jnp.int32, (cols, 1), 0)
    taps = [pltpu.roll(x, shift + 1 - b, 1) for b in range(3)]
    edges = (jnp.where(col == 0, 0.0, taps[0]), taps[1], jnp.where(col == cols - 1, 0.0, taps[2]))
    packed = [jnp.concatenate([t[r] for t in edges], axis=1).astype(BF) for r in range(x.shape[0])]
    return packed, taps[1]


def split_dot(lhs, rhs):
    mid = lhs.shape[1] // 256 * 128
    return dot(lhs[:, :mid], rhs[:mid, :]) + dot(lhs[:, mid:], rhs[mid:, :])


def settle_body(channels, ends, own_a, own_b, wc, bias, o_first, o_rest):
    own = jnp.concatenate([own_a[...], own_b[...]], axis=1)
    low = jnp.where(ends[0] == 1, 0.0, own[-1:])
    packed, center = lines_of(jnp.concatenate([own[:-1], low], axis=0), WIN // 2)
    early = dot(jnp.concatenate(packed[:3], axis=1), wc[3 * LANES :, :])
    late = dot(jnp.concatenate(packed[1:], axis=1), wc[...])
    parts = [early[:, :LANES], early[:, LANES:], late[:, :LANES], late[:, LANES:]]
    rows = [center[r] + bias[...] + part for r, part in enumerate(parts)]
    o_first[...] = rows[0]
    for r in range(1, 4):
        o_rest[r - 1] = rows[r].T


def final_body(channels, ends, high_a, high_b, own_a, own_b, first_row, rest, wc, bias, o_hbm, out, sems):
    high = jnp.concatenate([high_a[...], high_b[...]], axis=1).astype(F32)
    own = jnp.concatenate([own_a[:1], own_b[:1]], axis=1)
    top = jnp.where(ends[1] == 1, 0.0, high[:1])
    packed, center = lines_of(jnp.concatenate([top, high[1:], own], axis=0), WIN // 2)
    width = center.shape[1]
    both = split_dot(jnp.concatenate([jnp.concatenate(packed[i : i + 4], axis=1) for i in (0, 2)], axis=0), wc[...])
    rows = []
    for r in range(4):
        j, v = divmod(r, 2)
        rows.append(center[1 + r] + bias[...] + both[j * width : (j + 1) * width, v * LANES : (v + 1) * LANES])
    rows.append(first_row[...] + dot(packed[4], wc[: 3 * LANES, :LANES]))
    y = jnp.stack([row.T for row in rows] + [rest[r] for r in range(3)], axis=0)
    copies = []
    n = sems.shape[0]
    step = channels // n
    for i in range(n):
        at = i * step
        out[0, at : at + step] = jnp.swapaxes(y[:, at : at + step], 0, 1).astype(BF)
        copy = pltpu.make_async_copy(out.at[0, at : at + step], o_hbm.at[0, at : at + step], sems.at[i])
        copy.start()
        copies.append(copy)
    for copy in copies:
        copy.wait()


def call(body, outs, *args, scratch=(), scalars=0, remote=0, away=False):
    vm = pl.BlockSpec(memory_space=pltpu.VMEM)
    sm = pl.BlockSpec(memory_space=pltpu.SMEM)
    hbm = pl.BlockSpec(memory_space=pltpu.HBM)
    specs = [sm] * scalars + [hbm] * remote
    run = pl.pallas_call(
        body,
        out_shape=[jax.ShapeDtypeStruct(s, d) for s, d in outs],
        in_specs=specs + [vm] * (len(args) - len(specs)),
        out_specs=[hbm if away else vm] * len(outs),
        scratch_shapes=list(scratch),
        compiler_params=pltpu.CompilerParams(vmem_limit_bytes=24 * 1024 * 1024),
    )
    args = [pltpu.with_memory_space_constraint(a, pltpu.HBM) if i < scalars + remote and i >= scalars else a for i, a in enumerate(args)]
    return run(*args)


def section(frames, *params):
    ln_gain, gate_weight = params[0], params[3]
    _, channels, rows, cols = frames.shape
    layers = ln_gain.shape[0]
    hp = up(gate_weight.shape[2])
    tiles, depth = lax.axis_size("tile"), lax.axis_size("tm")
    where = lax.axis_index("tile")
    ends = jnp.stack([where == tiles - 1, where == 0]).astype(jnp.int32)
    axes = ("tile", "tm")

    def odd(f):
        return (f + 1) % depth if f % 2 else (f - 1) % depth

    def send(x, target):
        pairs = []
        for t in range(tiles):
            for f in range(depth):
                to_t, to_f = target(t, f)
                pairs.append((t * depth + f, to_t * depth + to_f))
        return lax.ppermute(x, axes, pairs)

    def bind(body, *extra):
        def wrapped(*refs):
            return body(channels, *extra, *refs)

        wrapped.__name__ = body.__name__
        return wrapped

    count = cols // WIN
    first = count // 2 + LEAD
    rest = count - first
    keep = rows // 2 + 1
    size = rows * WIN
    dma = pltpu.SemaphoreType.DMA
    parts = [-(-first // 2) + 1, first // 2 - 1, rest]
    x, *xs = call(
        bind(norm_body),
        [((count, size, LANES), F32)] + [((n, size, LANES), BF) for n in parts] + [(p.shape, p.dtype) for p in params],
        frames, *params,
        scratch=[pltpu.VMEM(frames.shape, BF), dma((1 + len(params),))],
        remote=1 + len(params),
    )
    xs, params = xs[: len(parts)], xs[len(parts) :]
    far = [send(part, lambda t, f: (t, f ^ 1)) for part in xs]
    q, k, *sets = call(bind(weights_body),
        [((count, size, LANES), BF), ((count, size, LANES), BF)]
        + [
            ((2, LANES), F32),
            ((LANES, 2 * LANES), BF),
            ((LANES, LANES), BF),
            ((LANES, LANES), BF),
            ((LANES, 2 * hp), BF),
            ((hp, LANES), BF),
            ((12 * LANES, 2 * LANES), BF),
            ((1, LANES), F32),
        ]
        * layers,
        *params, *xs,
    )

    gain, qk, vt, wo, wgu, wd, wc, bias = zip(*[sets[8 * l : 8 * l + 8] for l in range(layers)])

    def buf(n):
        return pltpu.VMEM((rows, n * WIN, LANES), F32)

    def piece(n, dtype=BF):
        return ((keep, n * WIN, LANES), dtype)

    inner = (gain[0], qk[0], vt[0], wo[0], wgu[0], wd[0])

    def thin(n):
        return (packed_rows(piece(n)[0], channels), BF)

    early = call(
        bind(layer0_first), [piece(parts[0], F32), piece(parts[0])],
        far[0], xs[0], x, q, k, *inner, scratch=[buf(parts[0])],
    )
    fed_a, low, low_a, high_a = call(
        bind(layer0_middle, parts[0]), [piece(first, F32), piece(first), thin(first), thin(first)],
        far[1], xs[1], x, q, k, *inner, *early, scratch=[buf(parts[1])],
    )
    far_high_a = send(high_a, lambda t, f: (t, odd(f)))
    far_low_a = send(low_a, lambda t, f: ((t - 1) % tiles, odd(f)))
    fed_b, low_b, high_b, low = call(bind(layer0_last, first), [piece(rest, F32), thin(rest), thin(rest), piece(count)],
        far[2], xs[2], x, q, k, *inner, low, scratch=[buf(rest)],
    )
    below = send(low, lambda t, f: ((t - 1) % tiles, f))
    far_high_b = send(high_b, lambda t, f: (t, odd(f)))
    far_low_b = send(low_b, lambda t, f: ((t - 1) % tiles, odd(f)))
    whole = (count, size, LANES)
    x, xn, q, k = call(bind(own1_body), [(whole, F32), (whole, BF), (whole, BF), (whole, BF)],
        ends, fed_a, fed_b, below, wc[0], bias[0], gain[1], qk[1], scalars=1,
    )
    inner = (wc[0], bias[0], gain[0], gain[1], qk[1], vt[1], wo[1], wgu[1], wd[1])
    half = first - 1
    own_a, send_a = call(bind(layer1_first), [piece(half, F32), piece(half)],
        ends, far_high_a, far_low_a, xn, x, q, k, *inner, scratch=[buf(half)], scalars=1,
    )
    above_a = send(send_a, lambda t, f: ((t + 1) % tiles, f))
    own_b, send_b = call(bind(layer1_second), [piece(count - half, F32), piece(count - half)],
        ends, far_high_a, far_low_a, far_high_b, far_low_b, xn, x, q, k, *inner, scratch=[buf(count - half)], scalars=1,
    )
    above_b = send(send_b, lambda t, f: ((t + 1) % tiles, f))
    first_row, rest = call(
        bind(settle_body), [((cols, LANES), F32), ((rows // 2 - 1, LANES, cols), F32)],
        ends, own_a, own_b, wc[1], bias[1], scalars=1,
    )
    (out,) = call(bind(final_body), [((1, channels, rows, cols), BF)], ends, above_a, above_b, own_a, own_b, first_row, rest, wc[1], bias[1],
        scratch=[pltpu.VMEM(frames.shape, BF), dma((5,))], scalars=1, away=True,
    )
    return out


def solution(mesh):
    in_specs = (P(("clips", "tm"), None, "tile", None), P(), P(), P(), P(), P(), P(), P(), P())
    out_specs = P(("clips", "tm"), None, "tile", None)
    return jax.shard_map(section, mesh=mesh, in_specs=in_specs, out_specs=out_specs, check_vma=False)
```

```python
import jax
import jax.numpy as jnp
from jax import lax
from jax.experimental import pallas as pl
from jax.experimental.pallas import tpu as pltpu
from jax.sharding import PartitionSpec as P


HEADS = 6
HD = 20
WIN = 8
LANES = 128
GROUP = 12
LEAD = 3
BF = jnp.bfloat16
F32 = jnp.float32
NT = (((1,), (1,)), ((), ()))


def up(n):
    return -(-n // LANES) * LANES


def dot(a, b):
    return jnp.dot(a, b, preferred_element_type=F32)


def dot_nt(a, b):
    return lax.dot_general(a, b, NT, preferred_element_type=F32)


def norm(x, gain, channels):
    lane = lax.broadcasted_iota(jnp.int32, x.shape, x.ndim - 1)
    mean = jnp.sum(x, axis=-1, keepdims=True) * (1.0 / channels)
    center = jnp.where(lane < channels, x - mean, 0.0)
    spread = jnp.sum(center * center, axis=-1, keepdims=True) * (1.0 / channels)
    return center * lax.rsqrt(spread + 1e-05) * gain


def to_positions(ref):
    x = ref[0].astype(F32)
    channels, rows, cols = x.shape
    x = jnp.concatenate([x, jnp.zeros((LANES - channels, rows, cols), F32)], axis=0)
    x = jnp.swapaxes(x, 0, 1)
    return jnp.stack([x[r].T for r in range(rows)], axis=0)


def windows(x):
    rows, cols, lanes = x.shape
    x = x.reshape(rows, cols // WIN, WIN, lanes)
    return jnp.swapaxes(x, 0, 1).reshape(cols // WIN, rows * WIN, lanes)


def unwindows(x, rows):
    count, _, lanes = x.shape
    x = jnp.swapaxes(x.reshape(count, rows, WIN, lanes), 0, 1)
    return x.reshape(rows, count * WIN, lanes)


def pad2(x, rows, cols):
    x = x.astype(F32)
    if x.shape[1] < cols:
        x = jnp.concatenate([x, jnp.zeros((x.shape[0], cols - x.shape[1]), F32)], axis=1)
    if x.shape[0] < rows:
        x = jnp.concatenate([x, jnp.zeros((rows - x.shape[0], cols), F32)], axis=0)
    return x


def norm_body(channels, x_hbm, *refs):
    x_ref, sems = refs[-2:]
    n = sems.shape[0] - 1
    params, o_x, o_parts, local = refs[:n], refs[n], refs[n + 1 : -2 - n], refs[-2 - n : -2]
    first = [pltpu.make_async_copy(x_hbm, x_ref, sems.at[n]), pltpu.make_async_copy(params[0], local[0], sems.at[0])]
    later = [pltpu.make_async_copy(params[i], local[i], sems.at[i]) for i in range(1, n)]
    for copy in first + later:
        copy.start()
    for copy in first:
        copy.wait()
    x = windows(to_positions(x_ref))
    o_x[...] = x
    xn = norm(x, pad2(local[0][0], 2, LANES)[:1], channels).astype(BF)
    at = 0
    for part in o_parts:
        part[...] = xn[at : at + part.shape[0]]
        at += part.shape[0]
    for copy in later:
        copy.wait()


def weights_body(channels, *refs):
    gain, qkv, out, gate, upw, down, conv, bias = refs[:8]
    layers = out.shape[0]
    xs, (o_q, o_k), outs = refs[8 : -2 - 8 * layers], refs[-2 - 8 * layers : -8 * layers], refs[-8 * layers :]
    hp = up(gate.shape[2])
    for l in range(layers):
        o_gain, o_qk, o_vt, o_out, o_gu, o_down, o_conv, o_bias = outs[8 * l : 8 * l + 8]
        o_gain[...] = pad2(gain[l], 2, LANES)
        o_bias[...] = pad2(bias[l : l + 1], 1, LANES)
        w = qkv[l].astype(F32)
        wq = pad2(w[:, :channels], LANES, LANES).astype(BF)
        wk = pad2(w[:, channels : 2 * channels], LANES, LANES).astype(BF)
        o_qk[:, :LANES] = wq
        o_qk[:, LANES:] = wk
        o_vt[...] = pad2(w[:, 2 * channels :], LANES, LANES).T.astype(BF)
        o_out[...] = pad2(out[l], LANES, LANES).astype(BF)
        o_gu[:, :hp] = pad2(gate[l], LANES, hp).astype(BF)
        o_gu[:, hp:] = pad2(upw[l], LANES, hp).astype(BF)
        o_down[...] = pad2(down[l], hp, LANES).astype(BF)
        blank = jnp.zeros((3 * LANES, LANES), BF)
        o_conv[3 * 3 * LANES :, :LANES] = blank
        o_conv[: 3 * LANES, LANES:] = blank
        for tap in range(9):
            a, b = divmod(tap, 3)
            piece = pad2(conv[l, tap], LANES, LANES).astype(BF)
            for v in range(2):
                at = ((a + v) * 3 + b) * LANES
                o_conv[at : at + LANES, v * LANES : (v + 1) * LANES] = piece
        if l == 0:
            project(jnp.concatenate([part[...] for part in xs], axis=0), jnp.concatenate([wq, wk], axis=1), o_q, o_k)


def project(xn, qk, o_q, o_k):
    count, size, _ = xn.shape
    both = dot(xn.reshape(count * size, LANES), qk).astype(BF)
    o_q[...] = both[:, :LANES].reshape(count, size, LANES)
    o_k[...] = both[:, LANES:].reshape(count, size, LANES)


def pieces(count):
    n = -(-count // GROUP)
    edges = [count * i // n for i in range(n + 1)]
    return [(a, b - a) for a, b in zip(edges, edges[1:])]


def pipeline(stages, total):
    held = [None] * (len(stages) + 1)
    for step in range(total + len(stages) - 1):
        for i in reversed(range(len(stages))):
            if 0 <= step - i < total:
                held[i + 1] = stages[i](step - i, held[i])


def mutual(channels, base, count, far, own, x_ref, q_ref, k_ref, gain, qk, vt, wo, wgu, wd, emit):
    size = x_ref.shape[1]
    hp = wd.shape[0]
    head_of = lax.broadcasted_iota(jnp.int32, (size, LANES), 1) // HD
    sub = lax.broadcasted_iota(jnp.int32, (LANES, LANES), 0) // HD
    half = lax.broadcasted_iota(jnp.int32, (LANES, LANES), 1) // size
    valid = (sub % 2 == half) & (sub < HEADS)
    scale = HD ** (-0.5) * 1.4426950408889634
    cuts = pieces(count)

    def fetch(g, _):
        at, n = cuts[g]
        fn = far(at, n)
        return fn, dot(fn.reshape(n * size, LANES), qk[:, LANES:]).astype(BF).reshape(n, size, LANES)

    def scores(g, state):
        fn, fk = state
        at, n = cuts[g]
        both = [jnp.concatenate([own[at + i], fn[i]], axis=0) for i in range(n)]
        vals = []
        for i in range(0, n, 2):
            pair = both[i : i + 2]
            v = dot_nt(vt[...], jnp.concatenate(pair, axis=0)).astype(BF)
            vals += [v[:, 2 * size * j : 2 * size * (j + 1)] for j in range(len(pair))]
        out = []
        for i in range(n):
            keys = jnp.concatenate([k_ref[base + at + i], fk[i]], axis=0)
            q = q_ref[base + at + i]
            qm = jnp.concatenate([jnp.where(head_of == h, q, jnp.zeros_like(q)) for h in range(HEADS)], axis=0)
            out.append((vals[i], dot_nt(keys, qm)))
        return out

    def attend(g, state):
        out = []
        for vals, s in state:
            top = jnp.max(s, axis=0, keepdims=True)
            p = jnp.exp2((s - top) * scale)
            p = (p * (1.0 / jnp.sum(p, axis=0, keepdims=True))).astype(BF)
            cut = 4 * HD
            out.append((dot(vals[:cut], p[:, : 4 * size]), dot(vals[cut:], p[:, 4 * size :])))
        return out

    def merge(g, state):
        mixed = []
        for front, back in state:
            two = 2 * HD
            r = jnp.concatenate([front[:two, :LANES], front[two:, LANES:], back], axis=0)
            r = jnp.where(valid, r, 0.0).T
            mixed.append(r[:size] + r[size:])
        mixed = jnp.concatenate(mixed, axis=0).astype(BF)
        at, n = cuts[g]
        return x_ref[base + at : base + at + n].reshape(n * size, LANES) + dot(mixed, wo[...])

    def widen(g, att):
        nf = norm(att, gain[1:2], channels).astype(BF)
        return att, dot(nf, wgu[...])

    def narrow(g, state):
        att, gu = state
        gate = gu[:, :hp]
        act = 0.5 * gate * (1.0 + lax.erf(gate * (0.5**0.5))) * gu[:, hp:]
        fed = att + dot(act.astype(BF), wd[...])
        at, n = cuts[g]
        emit(at, fed.reshape(n, size, LANES))

    pipeline([fetch, scores, attend, merge, widen, narrow], len(cuts))


def conv_cols(x, skip, origin, cols, edge, wc, bias):
    n = x.shape[1] - 2 * skip
    taps = [x[:, skip - 1 + b : skip - 1 + b + n] for b in range(3)]
    return conv_taps(taps, origin, cols, edge, wc, bias)


def conv_taps(taps, origin, cols, edge, wc, bias):
    center = taps[1]
    rows, width = center.shape[0] - 2, center.shape[1]
    col = (lax.broadcasted_iota(jnp.int32, (width, 1), 0) + origin) % cols
    parts = []
    for b, moved in enumerate(taps):
        if b != 1:
            moved = jnp.where(col == (0 if b == 0 else cols - 1), 0.0, moved)
        parts.append(moved)
    lines = [jnp.concatenate([p[r] for p in parts], axis=1) for r in range(rows + 2)]
    packed = [line.astype(BF) for line in lines]
    blocks = []
    for j in range(rows // 2):
        four = packed[2 * j : 2 * j + 4]
        if edge is not None:
            last, at = edge
            if 2 * j + 1 == at - 1:
                four[3] = jnp.where(last, 0.0, lines[2 * j + 3]).astype(BF)
            if 2 * j == at:
                four[0] = jnp.where(last, 0.0, lines[2 * j]).astype(BF)
        blocks.append(jnp.concatenate(four, axis=1))
    if width == cols:
        lhs = jnp.concatenate(blocks, axis=0)
        mid = lhs.shape[1] // 2
        both = dot(lhs[:, :mid], wc[:mid, :]) + dot(lhs[:, mid:], wc[mid:, :])
    else:
        mid = len(blocks) // 2
        both = [dot(jnp.concatenate(b, axis=0), wc[...]) for b in (blocks[:mid], blocks[mid:])]
        both = jnp.concatenate(both, axis=0)
    out = []
    for r in range(rows):
        j, v = divmod(r, 2)
        part = both[j * width : (j + 1) * width, v * LANES : (v + 1) * LANES]
        out.append(center[1 + r] + bias[...] + part)
    return jnp.stack(out, axis=0)


def packing(groups, channels):
    spare = LANES - channels
    if spare == 0 or channels % spare:
        return 0, 1
    per = channels // spare
    return groups // (per + 1), per


def packed_rows(shape, channels):
    groups = shape[0] * shape[1] // WIN
    return ((groups - packing(groups, channels)[0]) * WIN, LANES)


def pack(x, channels):
    groups = x.shape[0] * x.shape[1] // WIN
    extra, per = packing(groups, channels)
    x = x.reshape(groups, WIN, LANES)
    lane = lax.broadcasted_iota(jnp.int32, (WIN, LANES), 1)
    out = []
    for c in range(groups - extra):
        e, i = divmod(c, per)
        line = x[c]
        if e < extra:
            turn = (channels - (LANES - channels) * i) % LANES
            moved = pltpu.roll(x[groups - extra + e], turn, 1) if turn else x[groups - extra + e]
            line = jnp.where(lane < channels, line, moved)
        out.append(line)
    return jnp.concatenate(out, axis=0).astype(BF)


def unpack(y, rows, channels):
    y = y.astype(F32).reshape(-1, WIN, LANES)
    groups = next(g for g in range(y.shape[0], 2 * y.shape[0] + 1) if g - packing(g, channels)[0] == y.shape[0] and g % rows == 0)
    extra, per = packing(groups, channels)
    spare = LANES - channels
    lane = lax.broadcasted_iota(jnp.int32, (WIN, LANES), 1)
    out, tails = [], []
    for c in range(groups - extra):
        e, i = divmod(c, per)
        if e >= extra:
            out.append(y[c])
            continue
        out.append(jnp.where(lane < channels, y[c], 0.0))
        turn = (spare * i - channels) % LANES
        moved = pltpu.roll(y[c], turn, 1) if turn else y[c]
        if i == 0:
            tails.append(jnp.where(lane < spare, moved, 0.0))
        else:
            tails[e] = jnp.where((lane >= spare * i) & (lane < spare * (i + 1)), moved, tails[e])
    return jnp.stack(out + tails, axis=0).reshape(rows, groups // rows * WIN, LANES)


def collect(buf):
    def emit(at, fed):
        buf[:, at * WIN : (at + fed.shape[0]) * WIN, :] = unwindows(fed, buf.shape[0])

    return emit


def layer0_first(channels, far, own, x_ref, q_ref, k_ref, gain, qk, vt, wo, wgu, wd, o_fed, o_low, buf):
    rows, keep = buf.shape[0], o_low.shape[0]
    mutual(channels, 0, far.shape[0], lambda at, n: far[at : at + n], own, x_ref, q_ref, k_ref, gain, qk, vt, wo, wgu, wd, collect(buf))
    o_fed[...] = buf[rows - keep :]
    o_low[...] = buf[:keep].astype(BF)


def layer0_middle(channels, base, far, own, x_ref, q_ref, k_ref, gain, qk, vt, wo, wgu, wd, fed_a, low_a, o_fed, o_low, o_plow, o_phigh, buf):
    rows, keep = buf.shape[0], o_low.shape[0]
    mutual(channels, base, far.shape[0], lambda at, n: far[at : at + n], own, x_ref, q_ref, k_ref, gain, qk, vt, wo, wgu, wd, collect(buf))
    fed = jnp.concatenate([fed_a[...], buf[rows - keep :]], axis=1)
    low = jnp.concatenate([low_a[...].astype(F32), buf[:keep]], axis=1)
    o_fed[...] = fed
    o_low[...] = low.astype(BF)
    o_plow[...] = pack(low, channels)
    o_phigh[...] = pack(fed, channels)


def layer0_last(channels, base, far, own, x_ref, q_ref, k_ref, gain, qk, vt, wo, wgu, wd, low_a, o_fed, o_plow, o_phigh, o_low, buf):
    rows, keep = buf.shape[0], o_low.shape[0]
    mutual(channels, base, far.shape[0], lambda at, n: far[at : at + n], own, x_ref, q_ref, k_ref, gain, qk, vt, wo, wgu, wd, collect(buf))
    fed, low = buf[rows - keep :], buf[:keep]
    o_fed[...] = fed
    o_plow[...] = pack(low, channels)
    o_phigh[...] = pack(fed, channels)
    first = base * WIN
    o_low[:, :first, :] = low_a[...]
    o_low[:, first:, :] = low.astype(BF)


def own1_body(channels, last, fed_a, fed_b, low, wc, bias, gain, qk, o_x, o_xn, o_q, o_k):
    high = jnp.concatenate([fed_a[...], fed_b[...]], axis=1)
    x = jnp.concatenate([high, low[...].astype(F32)], axis=0)
    cols = x.shape[1]
    x = jnp.concatenate([x, x[:, :WIN]], axis=1)
    cuts = [(0, cols // WIN)]

    def mix(g, _):
        at, n = cuts[g]
        part = x[:, at * WIN : (at + n + 1) * WIN]
        return windows(conv_cols(part, WIN // 2, at * WIN + WIN // 2, cols, (lax.axis_index("tile") == last, WIN // 2), wc, bias))

    def finish(g, part):
        at, n = cuts[g]
        o_x[at : at + n] = part
        xn = norm(part, gain[0:1], channels).astype(BF)
        o_xn[at : at + n] = xn
        project(xn, qk[...], o_q.at[at : at + n], o_k.at[at : at + n])

    pipeline([mix, finish], len(cuts))


def far_normed(channels, last, x, base, cols, wc, bias, gain):
    def far(at, n):
        part = x[:, at * WIN : (at + n + 1) * WIN]
        part = conv_cols(part, WIN // 2, base + at * WIN + WIN // 2, cols, (lax.axis_index("tile") == last, WIN // 2), wc, bias)
        return norm(windows(part), gain[0:1], channels).astype(BF)

    return far


def layer1_first(channels, last, high, low, xn_ref, x_ref, q_ref, k_ref, wc, bias, gain0, gain, qk, vt, wo, wgu, wd, o_own, o_send, buf):
    rows, keep = buf.shape[0], o_own.shape[0]
    x = jnp.concatenate([unpack(high[...], keep, channels), unpack(low[...], keep, channels)], axis=0)
    count = buf.shape[1] // WIN
    far = far_normed(channels, last, x, 0, x_ref.shape[0] * WIN, wc, bias, gain)
    mutual(channels, 0, count, far, xn_ref, x_ref, q_ref, k_ref, gain, qk, vt, wo, wgu, wd, collect(buf))
    o_own[...] = buf[:keep]
    o_send[...] = buf[rows - keep :].astype(BF)


def layer1_second(channels, last, high_a, low_a, high_b, low_b, xn_ref, x_ref, q_ref, k_ref, wc, bias, gain0, gain, qk, vt, wo, wgu, wd, o_own, o_send, buf):
    keep = o_own.shape[0]
    xa = jnp.concatenate([unpack(part[...], keep, channels) for part in (high_a, low_a)], axis=0)
    xb = jnp.concatenate([unpack(part[...], keep, channels) for part in (high_b, low_b)], axis=0)
    cols = x_ref.shape[0] * WIN
    base = cols - buf.shape[1]
    x = jnp.concatenate([xa[:, base:], xb, xa[:, :WIN]], axis=1)
    rows, at, count = buf.shape[0], base // WIN, buf.shape[1] // WIN
    far = far_normed(channels, last, x, base, cols, wc, bias, gain)
    mutual(channels, at, count, far, xn_ref.at[at:], x_ref, q_ref, k_ref, gain, qk, vt, wo, wgu, wd, collect(buf))
    o_own[...] = buf[:keep]
    o_send[...] = buf[rows - keep :].astype(BF)


def lines_of(x, shift):
    cols = x.shape[1]
    col = lax.broadcasted_iota(jnp.int32, (cols, 1), 0)
    taps = [pltpu.roll(x, shift + 1 - b, 1) for b in range(3)]
    edges = (jnp.where(col == 0, 0.0, taps[0]), taps[1], jnp.where(col == cols - 1, 0.0, taps[2]))
    packed = [jnp.concatenate([t[r] for t in edges], axis=1).astype(BF) for r in range(x.shape[0])]
    return packed, taps[1]


def split_dot(lhs, rhs):
    mid = lhs.shape[1] // 256 * 128
    return dot(lhs[:, :mid], rhs[:mid, :]) + dot(lhs[:, mid:], rhs[mid:, :])


def settle_body(channels, last, own_a, own_b, wc, bias, o_first, o_rest):
    own = jnp.concatenate([own_a[...], own_b[...]], axis=1)
    low = jnp.where(lax.axis_index("tile") == last, 0.0, own[-1:])
    packed, center = lines_of(jnp.concatenate([own[:-1], low], axis=0), WIN // 2)
    early = dot(jnp.concatenate(packed[:3], axis=1), wc[3 * LANES :, :])
    late = dot(jnp.concatenate(packed[1:], axis=1), wc[...])
    parts = [early[:, :LANES], early[:, LANES:], late[:, :LANES], late[:, LANES:]]
    rows = [center[r] + bias[...] + part for r, part in enumerate(parts)]
    o_first[...] = rows[0]
    for r in range(1, 4):
        o_rest[r - 1] = rows[r].T


def final_body(channels, last, high_a, high_b, own_a, own_b, first_row, rest, wc, bias, o_hbm, out, sems):
    high = jnp.concatenate([high_a[...], high_b[...]], axis=1).astype(F32)
    own = jnp.concatenate([own_a[:1], own_b[:1]], axis=1)
    top = jnp.where(lax.axis_index("tile") == 0, 0.0, high[:1])
    packed, center = lines_of(jnp.concatenate([top, high[1:], own], axis=0), WIN // 2)
    width = center.shape[1]
    both = split_dot(jnp.concatenate([jnp.concatenate(packed[i : i + 4], axis=1) for i in (0, 2)], axis=0), wc[...])
    rows = []
    for r in range(4):
        j, v = divmod(r, 2)
        rows.append(center[1 + r] + bias[...] + both[j * width : (j + 1) * width, v * LANES : (v + 1) * LANES])
    rows.append(first_row[...] + dot(packed[4], wc[: 3 * LANES, :LANES]))
    y = jnp.stack([row.T for row in rows] + [rest[r] for r in range(3)], axis=0)
    copies = []
    n = sems.shape[0]
    step = channels // n
    for i in range(n):
        at = i * step
        out[0, at : at + step] = jnp.swapaxes(y[:, at : at + step], 0, 1).astype(BF)
        copy = pltpu.make_async_copy(out.at[0, at : at + step], o_hbm.at[0, at : at + step], sems.at[i])
        copy.start()
        copies.append(copy)
    for copy in copies:
        copy.wait()


def call(body, outs, *args, scratch=(), scalars=0, remote=0, away=False):
    vm = pl.BlockSpec(memory_space=pltpu.VMEM)
    sm = pl.BlockSpec(memory_space=pltpu.SMEM)
    hbm = pl.BlockSpec(memory_space=pltpu.HBM)
    specs = [sm] * scalars + [hbm] * remote
    run = pl.pallas_call(
        body,
        out_shape=[jax.ShapeDtypeStruct(s, d) for s, d in outs],
        in_specs=specs + [vm] * (len(args) - len(specs)),
        out_specs=[hbm if away else vm] * len(outs),
        scratch_shapes=list(scratch),
        compiler_params=pltpu.CompilerParams(vmem_limit_bytes=24 * 1024 * 1024),
    )
    args = [pltpu.with_memory_space_constraint(a, pltpu.HBM) if i < scalars + remote and i >= scalars else a for i, a in enumerate(args)]
    return run(*args)


def section(frames, *params):
    ln_gain, gate_weight = params[0], params[3]
    _, channels, rows, cols = frames.shape
    layers = ln_gain.shape[0]
    hp = up(gate_weight.shape[2])
    tiles, depth = lax.axis_size("tile"), lax.axis_size("tm")
    last_tile = tiles - 1
    axes = ("tile", "tm")

    def odd(f):
        return (f + 1) % depth if f % 2 else (f - 1) % depth

    def send(x, target):
        pairs = []
        for t in range(tiles):
            for f in range(depth):
                to_t, to_f = target(t, f)
                pairs.append((t * depth + f, to_t * depth + to_f))
        return lax.ppermute(x, axes, pairs)

    def bind(body, *extra):
        def wrapped(*refs):
            return body(channels, *extra, *refs)

        wrapped.__name__ = body.__name__
        return wrapped

    count = cols // WIN
    first = count // 2 + LEAD
    rest = count - first
    keep = rows // 2 + 1
    size = rows * WIN
    dma = pltpu.SemaphoreType.DMA
    parts = [-(-first // 2) + 1, first // 2 - 1, rest]
    x, *xs = call(
        bind(norm_body),
        [((count, size, LANES), F32)] + [((n, size, LANES), BF) for n in parts] + [(p.shape, p.dtype) for p in params],
        frames, *params,
        scratch=[pltpu.VMEM(frames.shape, BF), dma((1 + len(params),))],
        remote=1 + len(params),
    )
    xs, params = xs[: len(parts)], xs[len(parts) :]
    far = [send(part, lambda t, f: (t, f ^ 1)) for part in xs]
    q, k, *sets = call(bind(weights_body),
        [((count, size, LANES), BF), ((count, size, LANES), BF)]
        + [
            ((2, LANES), F32),
            ((LANES, 2 * LANES), BF),
            ((LANES, LANES), BF),
            ((LANES, LANES), BF),
            ((LANES, 2 * hp), BF),
            ((hp, LANES), BF),
            ((12 * LANES, 2 * LANES), BF),
            ((1, LANES), F32),
        ]
        * layers,
        *params, *xs,
    )

    gain, qk, vt, wo, wgu, wd, wc, bias = zip(*[sets[8 * l : 8 * l + 8] for l in range(layers)])

    def buf(n):
        return pltpu.VMEM((rows, n * WIN, LANES), F32)

    def piece(n, dtype=BF):
        return ((keep, n * WIN, LANES), dtype)

    inner = (gain[0], qk[0], vt[0], wo[0], wgu[0], wd[0])

    def thin(n):
        return (packed_rows(piece(n)[0], channels), BF)

    early = call(
        bind(layer0_first), [piece(parts[0], F32), piece(parts[0])],
        far[0], xs[0], x, q, k, *inner, scratch=[buf(parts[0])],
    )
    fed_a, low, low_a, high_a = call(
        bind(layer0_middle, parts[0]), [piece(first, F32), piece(first), thin(first), thin(first)],
        far[1], xs[1], x, q, k, *inner, *early, scratch=[buf(parts[1])],
    )
    far_high_a = send(high_a, lambda t, f: (t, odd(f)))
    far_low_a = send(low_a, lambda t, f: ((t - 1) % tiles, odd(f)))
    fed_b, low_b, high_b, low = call(bind(layer0_last, first), [piece(rest, F32), thin(rest), thin(rest), piece(count)],
        far[2], xs[2], x, q, k, *inner, low, scratch=[buf(rest)],
    )
    below = send(low, lambda t, f: ((t - 1) % tiles, f))
    far_high_b = send(high_b, lambda t, f: (t, odd(f)))
    far_low_b = send(low_b, lambda t, f: ((t - 1) % tiles, odd(f)))
    whole = (count, size, LANES)
    x, xn, q, k = call(bind(own1_body, last_tile), [(whole, F32), (whole, BF), (whole, BF), (whole, BF)],
        fed_a, fed_b, below, wc[0], bias[0], gain[1], qk[1],
    )
    inner = (wc[0], bias[0], gain[0], gain[1], qk[1], vt[1], wo[1], wgu[1], wd[1])
    half = first - 1
    own_a, send_a = call(bind(layer1_first, last_tile), [piece(half, F32), piece(half)],
        far_high_a, far_low_a, xn, x, q, k, *inner, scratch=[buf(half)],
    )
    above_a = send(send_a, lambda t, f: ((t + 1) % tiles, f))
    own_b, send_b = call(bind(layer1_second, last_tile), [piece(count - half, F32), piece(count - half)],
        far_high_a, far_low_a, far_high_b, far_low_b, xn, x, q, k, *inner, scratch=[buf(count - half)],
    )
    above_b = send(send_b, lambda t, f: ((t + 1) % tiles, f))
    first_row, rest = call(
        bind(settle_body, last_tile), [((cols, LANES), F32), ((rows // 2 - 1, LANES, cols), F32)],
        own_a, own_b, wc[1], bias[1],
    )
    (out,) = call(bind(final_body, last_tile), [((1, channels, rows, cols), BF)], above_a, above_b, own_a, own_b, first_row, rest, wc[1], bias[1],
        scratch=[pltpu.VMEM(frames.shape, BF), dma((5,))], away=True,
    )
    return out


def solution(mesh):
    in_specs = (P(("clips", "tm"), None, "tile", None), P(), P(), P(), P(), P(), P(), P(), P())
    out_specs = P(("clips", "tm"), None, "tile", None)
    return jax.shard_map(section, mesh=mesh, in_specs=in_specs, out_specs=out_specs, check_vma=False)
```
